512 devices in a mesh: leaf: 128 (over z, y, core), chan: 4 (over x).
Axes of the slice: x: 4, y: 8, z: 8, core: 2. Of those that a mesh axis runs over, the one named last changes fastest.
Arguments:
- features: bfloat16 [64, 524288], P(None, 'leaf'), may hold values from -6 to 6
- neighbours: int32 [27, 524288], P(None, 'leaf'), may hold values from -1 to 2048, as said below
- child_count: int32 [128], P('leaf'), may hold values from 1024 to 4096, as said below
- dest: int32 [65536], P('leaf'), may hold values from -1 to 65535, as said below
- conv_weight: bfloat16 [27, 64, 64], P(None, None, 'chan'), may hold values from -0.15625 to 0.15625
- merge_weight: bfloat16 [8, 64, 128], P(None, None, 'chan'), may hold values from -0.25 to 0.25
- parent_grad: bfloat16 [128, 65536], P('chan', 'leaf'), may hold values from -6 to 6
Outputs:
- parents: bfloat16 [128, 65536], P('chan', 'leaf')
- merge_weight_grad: float32 [8, 64, 128], P(None, None, 'chan')
The draws below stay inside these ranges and needn't reach their ends.
Inputs may be any that keep to these rules, and one draw needn't show every extreme that they name: `neighbours`: entry [k, r] is -1 where the neighbour is empty; else r + entry - 1024 is the index of a valid child octant, so the entry lies in 0 to 2048. Slots beyond a device's valid octants may hold entries too. Row 13 holds 1024 for every valid r. `child_count`: A multiple of 8; the valid child octants are the first ones of each device's 4096 slots; in every draw some device is full. `dest`: for parent slot g of device d, valid where g < child_count[d] / 8: t // 512 is the owner device and t % 512 = d * 4 + g % 4; the 4 slots with one value of g // 4 share an owner, and distinct such blocks of one device have distinct owners; -1 where g is not valid.
All inputs are finite; a program needn't handle non-finite values.
Results may differ from the reference program's by a relative error of at most 0.005.
Values may be sent and summed in bfloat16 or wider, within the bound.
No kernel may reach another device: no remote copies, remote signals or barrier semaphores. Data moves between devices by JAX's collectives and lax.ppermute only.
A program may use at most 64 MiB of HBM per device.

```python
import math
import jax
import jax.numpy as jnp
from jax import lax

C1 = 64
C2 = 128
TAPS = 27
KIDS = 8
PG = 512
CHILD = 4096
CAP = 4
HALO = 1024
N_LEAF = 128


def layout(key):
    base_key = jax.random.fold_in(key, 11)
    first_key = jax.random.fold_in(base_key, 1)
    second_key = jax.random.fold_in(base_key, 2)
    third_key = jax.random.fold_in(base_key, 3)
    groups = jax.random.randint(first_key, (N_LEAF,), PG // 4, PG + 1)
    full_device = jax.random.randint(second_key, (), 0, N_LEAF)
    device_ids = jnp.arange(N_LEAF)
    groups = jnp.where((device_ids == full_device) | (device_ids == N_LEAF - 2), PG, groups)
    shifts = jax.random.permutation(third_key, N_LEAF)
    return (groups.astype(jnp.int32), shifts.astype(jnp.int32))


def draw_child_count(key, part):
    groups, shifts = layout(key)
    return (groups * 8).astype(jnp.int32)


def draw_dest(key, part):
    groups, shifts = layout(key)
    slot_ids = jnp.arange(PG, dtype=jnp.int32)
    blocks = slot_ids // CAP
    within = slot_ids % CAP
    devices = jnp.arange(N_LEAF, dtype=jnp.int32)[:, None]
    owners = (devices + shifts[blocks][None, :]) % N_LEAF
    target = owners * PG + devices * CAP + within[None, :]
    living = slot_ids[None, :] < groups[:, None]
    return jnp.where(living, target, -1).reshape(N_LEAF * PG).astype(jnp.int32)


def draw_neighbours(key, part):
    groups, shifts = layout(key)
    counts = groups * 8
    total_rows = N_LEAF * CHILD
    row_ids = jnp.arange(total_rows, dtype=jnp.int32)
    offsets = jax.random.randint(jax.random.fold_in(key, 21), (TAPS, total_rows), -HALO, HALO + 1)
    centre = TAPS // 2
    offsets = offsets.at[centre].set(0)
    target = row_ids[None, :] + offsets
    inside = (target >= 0) & (target < total_rows)
    clipped = jnp.clip(target, 0, total_rows - 1)
    target_dev = clipped // CHILD
    target_loc = clipped - target_dev * CHILD
    living = target_loc < counts[target_dev]
    kept_mask = jax.random.randint(jax.random.fold_in(key, 22), (TAPS, total_rows), 0, 6) != 0
    kept_mask = kept_mask.at[centre].set(True)
    chosen = inside & living & kept_mask
    return jnp.where(chosen, offsets + HALO, -1).astype(jnp.int32)


def levels(key, extent, shards, low, top_value):
    def one(dim, parts):
        heights = jax.random.uniform(jax.random.fold_in(jax.random.fold_in(key, 6), dim), (parts,), jnp.float32, low / len(shards), top_value / len(shards))
        return jnp.repeat(jnp.exp(heights), extent[dim] // parts).reshape((-1,) + (1,) * (len(extent) - dim - 1))

    factor_of = one(*shards[0])
    for cut in shards[1:]:
        factor_of = factor_of * one(*cut)
    return factor_of


def noise(key, shape, deviation, limit, shards=(), kind=jnp.bfloat16):
    level = levels(key, shape, shards, -0.22, 0.18) if shards else 1.0
    drawn = jax.random.normal(key, shape, jnp.float32) * deviation * level
    return jnp.minimum(jnp.maximum(drawn, -limit), limit).astype(kind)


def setup_inputs(seed: int = 0) -> dict:
    arg_keys = jax.random.split(jax.random.key(seed), 8)
    return {
        "features": noise(arg_keys[0], (C1, N_LEAF * CHILD), 1.0, 6.0, ((1, 128),)),
        "neighbours": draw_neighbours(jax.random.fold_in(arg_keys[7], 71), 0),
        "child_count": draw_child_count(jax.random.fold_in(arg_keys[7], 71), 0),
        "dest": draw_dest(jax.random.fold_in(arg_keys[7], 71), 0),
        "conv_weight": noise(arg_keys[4], (TAPS, C1, C1), (TAPS * C1) ** -0.5, 0.15625, ((2, 4),)),
        "merge_weight": noise(arg_keys[5], (KIDS, C1, C2), (KIDS * C1) ** -0.5, 0.25, ((2, 4),)),
        "parent_grad": noise(arg_keys[6], (C2, N_LEAF * PG), 1.0, 6.0, ((0, 4), (1, 128))),
    }


def reference(features, neighbours, child_count, dest, conv_weight, merge_weight, parent_grad):
    conv_full = conv_weight.astype(jnp.float32)

    def device_block(device):
        offset_block = lax.dynamic_slice_in_dim(neighbours, device * CHILD, CHILD, 1)
        present = offset_block >= 0
        row_ids = device * CHILD + jnp.arange(CHILD, dtype=jnp.int32)
        global_index = row_ids[None, :] + offset_block - HALO
        safe_index = jnp.where(present, global_index, 0).astype(jnp.int32)
        gathered = features[:, safe_index] * present.astype(jnp.bfloat16)[None]
        pre_act = jnp.einsum('ckr,kco->or', gathered.astype(jnp.float32), conv_full)
        living = jnp.arange(CHILD, dtype=jnp.int32) < child_count[device]
        return (jnp.maximum(pre_act, 0.0) * living[None, :]).astype(jnp.bfloat16)
    stacked = lax.map(device_block, jnp.arange(N_LEAF, dtype=jnp.int32))
    hidden = jnp.moveaxis(stacked, 0, 1).reshape(C1, N_LEAF * CHILD)
    grouped = hidden.reshape(C1, N_LEAF * PG, KIDS).astype(jnp.float32)
    merged = jnp.einsum('cqk,kco->oq', grouped, merge_weight.astype(jnp.float32)).astype(jnp.bfloat16)
    living_group = dest >= 0
    slot_place = jnp.where(living_group, dest, N_LEAF * PG)
    parents = jnp.zeros((C2, N_LEAF * PG), jnp.bfloat16).at[:, slot_place].set(merged, mode='drop')
    fetched = parent_grad[:, jnp.where(living_group, dest, 0)] * living_group.astype(jnp.bfloat16)[None, :]
    weight_term = jnp.einsum('cqk,oq->kco', grouped, fetched.astype(jnp.float32))
    merge_weight_grad = weight_term / math.sqrt(KIDS * PG)
    return (parents, merge_weight_grad)
```

```python
import functools
import math

import jax
import jax.numpy as jnp
from jax import lax
from jax.experimental import pallas as pl
from jax.experimental.pallas import tpu as pltpu
from jax.sharding import PartitionSpec as P

KIDS = 8
HALO = 1024
BLOCK = 256
VMEM_BYTES = 48 << 20

BF16 = jnp.bfloat16
F32 = jnp.float32


def dot(a, b, contract):
    return lax.dot_general(a, b, ((contract[:1], contract[1:]), ((), ())), preferred_element_type=F32)


def iota(shape, dim):
    return lax.broadcasted_iota(jnp.int32, shape, dim)


def one_hot(hit):
    return jnp.where(hit, 1.0, 0.0).astype(BF16)


def conv_kernel(
    place_ref,
    features_ref,
    halo_ref,
    offsets_ref,
    weight0_ref,
    weight1_ref,
    weight2_ref,
    weight3_ref,
    out_ref,
    window,
    weight,
    low,
    high,
    gathered,
    swap,
):
    channel, valid_rows = place_ref[0], place_ref[1]
    step = pl.program_id(0)
    width = features_ref.shape[0]
    taps = weight0_ref.shape[0]
    part = weight0_ref.shape[1]
    chans = features_ref.shape[1] // HALO
    halo_pieces = HALO // BLOCK
    pieces = window.shape[0] // width
    reach = (2 * HALO) // BLOCK + 1

    @pl.when(step == 0)
    def _():
        for piece in range(pieces):
            at = channel * halo_pieces + piece - halo_pieces
            last = features_ref.shape[1] // BLOCK - 1
            inside = jnp.clip(at, 0, last) * BLOCK
            own = features_ref[:, pl.ds(pl.multiple_of(inside, BLOCK), BLOCK)]
            other = halo_ref[:, (piece % halo_pieces) * BLOCK : (piece % halo_pieces + 1) * BLOCK]
            outside = (at < 0) | (at > last)
            window[piece * width : (piece + 1) * width, :] = jnp.where(outside, other, own)
        for shift, ref in enumerate((weight0_ref, weight1_ref, weight2_ref, weight3_ref)):
            source = lax.rem(channel + chans - shift, chans)
            rows = pl.ds(pl.multiple_of(source * part, part), part)
            for tap in range(taps):
                weight[rows, tap * width : (tap + 1) * width] = ref[tap]
        row, lane = iota((BLOCK, BLOCK), 0), iota((BLOCK, BLOCK), 1)
        kid, slot, group = row & 7, (row >> 3) & 3, row >> 5
        swap[...] = one_hot(lane == kid * 32 + slot * 8 + group)

    offsets = offsets_ref[...]
    at = offsets + iota(offsets.shape, 1)
    low[...] = jnp.where(offsets >= 0, at & (BLOCK - 1), -1)
    high[...] = at >> 8
    first = pl.multiple_of(step * width, width)

    def tap_step(tap, carry):
        hit = one_hot(iota((BLOCK, BLOCK), 0) == low[pl.ds(tap, 1), :])
        found = dot(window[pl.ds(first, reach * width), :], hit, (1, 0))
        block = high[pl.ds(tap, 1), :]
        total = found[:width]
        for k in range(1, reach):
            total = jnp.where(block == k, found[k * width : (k + 1) * width], total)
        gathered[pl.ds(pl.multiple_of(tap * width, width), width), :] = total.astype(BF16)
        return carry

    lax.fori_loop(0, taps, tap_step, 0, unroll=3)
    pre_act = dot(weight[...], gathered[...], (1, 0))
    row = channel * HALO + step * BLOCK + iota((1, BLOCK), 1)
    hidden = jnp.where(row < valid_rows, jnp.maximum(pre_act, 0.0), 0.0).astype(BF16)
    spread = dot(hidden, swap[...], (1, 0))
    mine = (iota((width, 128), 1) >> 5) == step
    for kid in range(KIDS):
        half = spread[:, (kid // 4) * 128 : (kid // 4 + 1) * 128]
        moved = pltpu.roll(half, lax.rem(32 * step + 128 - 32 * (kid % 4), 128), axis=1)
        rows = slice(kid * width, (kid + 1) * width)
        out_ref[rows, :] = jnp.where(mine, moved, out_ref[rows, :].astype(F32)).astype(BF16)


def conv(place, features, halo, offsets, weights):
    width, rows = features.shape
    taps, part, _ = weights[0].shape
    quarter = HALO
    steps = quarter // BLOCK
    whole = lambda shape: pl.BlockSpec(shape, lambda b, place: (0,) * len(shape))
    return pl.pallas_call(
        conv_kernel,
        name="conv",
        out_shape=jax.ShapeDtypeStruct((KIDS * width, quarter // KIDS), BF16),
        grid_spec=pltpu.PrefetchScalarGridSpec(
            num_scalar_prefetch=1,
            grid=(steps,),
            in_specs=[
                whole((width, rows)),
                whole((width, HALO)),
                pl.BlockSpec((taps, BLOCK), lambda b, place: (0, place[0] * steps + b)),
                *[whole((taps, part, width))] * 4,
            ],
            out_specs=whole((KIDS * width, quarter // KIDS)),
            scratch_shapes=[
                pltpu.VMEM(((quarter + 2 * HALO) // BLOCK * width, BLOCK), BF16),
                pltpu.VMEM((4 * part, taps * width), BF16),
                pltpu.VMEM((taps, BLOCK), jnp.int32),
                pltpu.VMEM((taps, BLOCK), jnp.int32),
                pltpu.VMEM((taps * width, BLOCK), BF16),
                pltpu.VMEM((BLOCK, BLOCK), BF16),
            ],
        ),
        compiler_params=pltpu.CompilerParams(vmem_limit_bytes=VMEM_BYTES),
        cost_estimate=pl.CostEstimate(flops=8_000_000_000, bytes_accessed=2_000_000, transcendentals=0),
    )(place, features, halo, offsets, *weights)


def cut_kernel(grad_ref, out_ref):
    peers = out_ref.shape[0]
    slots = grad_ref.shape[1]
    grad = jnp.concatenate([grad_ref[...]] * 4, axis=0).astype(F32)
    keep = (iota(grad.shape, 1) & 3) == (iota(grad.shape, 0) >> 5)
    grad = jnp.where(keep, grad, 0.0).astype(BF16)
    place = one_hot((iota((peers, slots), 1) >> 2) == iota((peers, slots), 0))
    out_ref[...] = dot(place, grad, (1, 1))


def cut_to_owners(parent_grad, peers):
    return pl.pallas_call(
        cut_kernel,
        name="cut",
        out_shape=jax.ShapeDtypeStruct((peers, 128), F32),
    )(parent_grad)


def merge_kernel(owner_ref, hidden_ref, weight_ref, returned_ref, out_ref):
    peers = out_ref.shape[0]
    count = hidden_ref.shape[0]
    slots = owner_ref.shape[1]
    share = slots // count
    depth = hidden_ref.shape[1]
    place = one_hot(iota((peers, slots), 0) == owner_ref[...])
    own = ((iota((slots, 128), 0) >> 3) & 3) == (iota((slots, 128), 1) >> 5)
    fetched = jnp.where(own, dot(place, returned_ref[...].astype(BF16), (0, 0)), 0.0)
    fetched = fetched + pltpu.roll(fetched, 64, axis=1)
    fetched = fetched + pltpu.roll(fetched, 32, axis=1)
    fetched = fetched.astype(BF16)
    outbox = jnp.zeros((peers, 128), F32)
    grad = jnp.zeros((128, depth), F32)
    for piece in range(count):
        hidden = hidden_ref[piece]
        rows = slice(piece * share, (piece + 1) * share)
        merged = dot(hidden, weight_ref[...], (0, 0))
        merged = jnp.where(own[rows], merged, 0.0).astype(BF16)
        outbox = outbox + dot(place[:, rows], merged, (1, 0))
        grad = grad + dot(fetched[rows], hidden, (0, 1))
    out_ref[:, :128] = outbox
    for k in range(depth // 128):
        out_ref[k * 32 : (k + 1) * 32, 128:] = grad[:32, k * 128 : (k + 1) * 128]


def merge(owner, hidden, weight, returned, peers):
    return pl.pallas_call(
        merge_kernel,
        name="merge",
        out_shape=jax.ShapeDtypeStruct((peers, 256), F32),
        compiler_params=pltpu.CompilerParams(vmem_limit_bytes=VMEM_BYTES),
    )(owner, hidden, weight, returned)


def arrive_kernel(scale, arrived_ref, parents_ref, total_ref):
    peers = arrived_ref.shape[0]
    slots = parents_ref.shape[1]
    place = one_hot((iota((peers, slots), 1) >> 2) == iota((peers, slots), 0))
    spread = dot(arrived_ref[:, :128].astype(BF16), place, (0, 0))
    keep = (iota(spread.shape, 1) & 3) == (iota(spread.shape, 0) >> 5)
    spread = jnp.where(keep, spread, 0.0)
    parents = spread[:32] + spread[32:64] + spread[64:96] + spread[96:]
    parents_ref[...] = parents.astype(BF16)
    total = jnp.sum(arrived_ref[:, 128:], axis=0, keepdims=True) * scale
    total_ref[...] = jnp.broadcast_to(total, total_ref.shape)


def arrive(arrived, scale, slots):
    peers = arrived.shape[0]
    return pl.pallas_call(
        functools.partial(arrive_kernel, scale),
        name="arrive",
        out_shape=(
            jax.ShapeDtypeStruct((32, slots), BF16),
            jax.ShapeDtypeStruct((peers, 128), F32),
        ),
    )(arrived)


def exchange(array, axis):
    return lax.all_to_all(array, axis, 0, 0, tiled=True)


def per_device(features, neighbours, child_count, dest, conv_weight, merge_weight, parent_grad):
    chans, peers = lax.axis_size("chan"), lax.axis_size("leaf")
    width, rows = features.shape
    slots = parent_grad.shape[1]
    channel = lax.axis_index("chan")
    place = jnp.stack([channel, child_count[0]]).astype(jnp.int32)

    edge = jnp.where(channel == 0, features[:, rows - HALO :], features[:, :HALO])
    pairs = [(p * chans, (p + 1) * chans) for p in range(peers - 1)]
    pairs += [((p + 1) * chans + chans - 1, p * chans + chans - 1) for p in range(peers - 1)]
    halo = lax.ppermute(edge, ("leaf", "chan"), pairs)

    weight = jnp.swapaxes(conv_weight, 1, 2)
    weights = [weight]
    for shift in range(1, chans):
        ring = [(c, (c + shift) % chans) for c in range(chans)]
        weights.append(lax.ppermute(weight, "chan", ring))

    returned = exchange(cut_to_owners(parent_grad, peers), "leaf")

    owner = jnp.where(dest >= 0, dest // slots, -1)
    owner = owner.reshape(slots // 32, 8, 4).transpose(0, 2, 1).reshape(1, slots)
    merge_all = jnp.tile(merge_weight.reshape(KIDS * width, 32), (1, 4))

    hidden = conv(place, features, halo, neighbours, weights)
    hidden = exchange(jnp.broadcast_to(hidden[None], (chans, *hidden.shape)), "chan")
    outbox = merge(owner, hidden, merge_all, returned, peers)
    parents, total = arrive(exchange(outbox, "leaf"), 1.0 / math.sqrt(rows), slots)
    grad = exchange(total, "leaf")
    grad = grad.reshape(KIDS // 2, 32, 2, width).transpose(0, 2, 3, 1)
    return parents, grad.reshape(KIDS, width, 32)


def solution(mesh):
    in_specs = (
        P(None, "leaf"),
        P(None, "leaf"),
        P("leaf"),
        P("leaf"),
        P(None, None, "chan"),
        P(None, None, "chan"),
        P("chan", "leaf"),
    )
    out_specs = (P("chan", "leaf"), P(None, None, "chan"))
    return jax.shard_map(
        per_device, mesh=mesh, in_specs=in_specs, out_specs=out_specs, check_vma=False
    )
```

```python
import functools
import math

import jax
import jax.numpy as jnp
from jax import lax
from jax.experimental import pallas as pl
from jax.experimental.pallas import tpu as pltpu
from jax.sharding import Mesh, PartitionSpec as P

KIDS = 8
HALO = 1024
BLOCK = 256
VMEM_BYTES = 24 << 20
SMALL_BYTES = 8 << 20

BF16 = jnp.bfloat16
F32 = jnp.float32
LEAF = ("high", "low")


def dot(a, b, contract):
    return lax.dot_general(a, b, ((contract[:1], contract[1:]), ((), ())), preferred_element_type=F32)


def iota(shape, dim):
    return lax.broadcasted_iota(jnp.int32, shape, dim)


def one_hot(hit):
    return jnp.where(hit, 1.0, 0.0).astype(BF16)


def conv_kernel(
    place_ref,
    features_ref,
    halo_ref,
    offsets_ref,
    weight0_ref,
    weight1_ref,
    weight2_ref,
    weight3_ref,
    out_ref,
    window,
    weight,
    gathered,
    swap,
    piece,
):
    channel, valid_rows = place_ref[0], place_ref[1]
    width = features_ref.shape[0]
    taps = weight0_ref.shape[0]
    part = weight0_ref.shape[1]
    chans = features_ref.shape[1] // HALO
    halo_pieces = HALO // BLOCK
    pieces = window.shape[0] // width
    reach = (2 * HALO) // BLOCK + 1

    for i in range(pieces):
        at = channel * halo_pieces + i - halo_pieces
        last = features_ref.shape[1] // BLOCK - 1
        inside = jnp.clip(at, 0, last) * BLOCK
        own = features_ref[:, pl.ds(pl.multiple_of(inside, BLOCK), BLOCK)]
        other = halo_ref[:, (i % halo_pieces) * BLOCK : (i % halo_pieces + 1) * BLOCK]
        outside = (at < 0) | (at > last)
        window[i * width : (i + 1) * width, :] = jnp.where(outside, other, own)
    for shift, ref in enumerate((weight0_ref, weight1_ref, weight2_ref, weight3_ref)):
        source = lax.rem(channel + chans - shift, chans)
        rows = pl.ds(pl.multiple_of(source * part, part), part)
        for tap in range(taps):
            weight[rows, tap * width : (tap + 1) * width] = ref[tap]
    row, lane = iota((BLOCK, BLOCK), 0), iota((BLOCK, BLOCK), 1)
    kid, slot, group = row & 7, (row >> 3) & 3, row >> 5
    swap[...] = one_hot(lane == kid * 32 + slot * 8 + group)

    def one_step(step):
        offsets = offsets_ref[:, pl.ds(pl.multiple_of(channel * HALO + step * BLOCK, BLOCK), BLOCK)]
        at = offsets + iota(offsets.shape, 1)
        low = jnp.where(offsets >= 0, at & (BLOCK - 1), -1)
        high = at >> 8
        first = step * width
        base = slice(None)
        iota16 = lax.broadcasted_iota(jnp.int16, (BLOCK, BLOCK), 0)
        one16 = jnp.ones((BLOCK, BLOCK), BF16)
        zero16 = jnp.zeros((BLOCK, BLOCK), BF16)
        middle = taps // 2
        for tap in range(taps):
            rows = slice(tap * width, (tap + 1) * width)
            if tap == middle:
                centre = first + HALO // BLOCK * width
                gathered[rows, base] = window[pl.ds(centre, width), :]
                continue
            hit = jnp.where(iota16 == low[tap : tap + 1, :].astype(jnp.int16), one16, zero16)
            found = dot(window[pl.ds(first, reach * width), :], hit, (1, 0))
            block = high[tap : tap + 1, :]
            total = found[:width]
            for k in range(1, reach):
                total = jnp.where(block == k, found[k * width : (k + 1) * width], total)
            gathered[rows, base] = total.astype(BF16)

        def finish(step, columns):
            pre_act = dot(weight[...], gathered[:, columns], (1, 0))
            row = channel * HALO + step * BLOCK + iota((1, BLOCK), 1)
            hidden = jnp.where(row < valid_rows, jnp.maximum(pre_act, 0.0), 0.0).astype(BF16)
            spread = dot(hidden, swap[...], (1, 0))
            mine = (iota((width, 128), 1) >> 5) == step
            for kid in range(KIDS):
                half = spread[:, (kid // 4) * 128 : (kid // 4 + 1) * 128]
                moved = pltpu.roll(half, (32 * step + 128 - 32 * (kid % 4)) % 128, axis=1)
                rows = slice(kid * width, (kid + 1) * width)
                piece[rows, :] = jnp.where(mine, moved, piece[rows, :])

        finish(step, slice(None))
    for b in range(HALO // BLOCK):
        one_step(b)
    for peer in range(out_ref.shape[0]):
        out_ref[peer] = piece[...].astype(BF16)


def conv(place, features, halo, offsets, weights):
    width, rows = features.shape
    taps, part, _ = weights[0].shape
    quarter = HALO
    vmem = pl.BlockSpec(memory_space=pltpu.VMEM)
    return pl.pallas_call(
        conv_kernel,
        name="conv",
        out_shape=jax.ShapeDtypeStruct((len(weights), KIDS * width, quarter // KIDS), BF16),
        in_specs=[pl.BlockSpec(memory_space=pltpu.SMEM)] + [vmem] * 7,
        out_specs=vmem,
        scratch_shapes=[
            pltpu.VMEM(((quarter + 2 * HALO) // BLOCK * width, BLOCK), BF16),
            pltpu.VMEM((4 * part, taps * width), BF16),
            pltpu.VMEM((taps * width, BLOCK), BF16),
            pltpu.VMEM((BLOCK, BLOCK), BF16),
            pltpu.VMEM((KIDS * width, quarter // KIDS), F32),
        ],
        compiler_params=pltpu.CompilerParams(vmem_limit_bytes=VMEM_BYTES),
        cost_estimate=pl.CostEstimate(flops=8_000_000_000, bytes_accessed=2_000_000, transcendentals=0),
    )(place, features, halo, offsets, *weights)


def cut_kernel(grad_ref, out_ref):
    peers = out_ref.shape[0]
    slots = grad_ref.shape[1]
    grad = jnp.concatenate([grad_ref[...]] * 4, axis=0).astype(F32)
    keep = (iota(grad.shape, 1) & 3) == (iota(grad.shape, 0) >> 5)
    grad = jnp.where(keep, grad, 0.0).astype(BF16)
    place = one_hot((iota((peers, slots), 1) >> 2) == iota((peers, slots), 0))
    out_ref[...] = dot(place, grad, (1, 1))


def cut_to_owners(parent_grad, peers):
    return pl.pallas_call(
        cut_kernel,
        name="cut",
        out_shape=jax.ShapeDtypeStruct((peers, 128), F32),
        compiler_params=pltpu.CompilerParams(vmem_limit_bytes=SMALL_BYTES),
    )(parent_grad)


def merge_kernel(owner_ref, hidden_ref, weight_ref, returned_ref, out_ref):
    peers = out_ref.shape[0]
    count = hidden_ref.shape[0]
    slots = owner_ref.shape[1]
    share = slots // count
    depth = hidden_ref.shape[1]
    place = one_hot(iota((peers, slots), 0) == owner_ref[...])
    own = ((iota((slots, 128), 0) >> 3) & 3) == (iota((slots, 128), 1) >> 5)
    fetched = jnp.where(own, dot(place, returned_ref[...].astype(BF16), (0, 0)), 0.0)
    fetched = fetched + pltpu.roll(fetched, 64, axis=1)
    fetched = fetched + pltpu.roll(fetched, 32, axis=1)
    fetched = fetched.astype(BF16)
    outbox = jnp.zeros((peers, 128), F32)
    grad = jnp.zeros((128, depth), F32)
    for piece in range(count):
        hidden = hidden_ref[piece]
        rows = slice(piece * share, (piece + 1) * share)
        merged = dot(hidden, weight_ref[...], (0, 0))
        merged = jnp.where(own[rows], merged, 0.0).astype(BF16)
        outbox = outbox + dot(place[:, rows], merged, (1, 0))
        grad = grad + dot(fetched[rows], hidden, (0, 1))
    out_ref[:, :128] = outbox
    for k in range(depth // 128):
        out_ref[k * 32 : (k + 1) * 32, 128:] = grad[:32, k * 128 : (k + 1) * 128]


def merge(owner, hidden, weight, returned, peers):
    return pl.pallas_call(
        merge_kernel,
        name="merge",
        out_shape=jax.ShapeDtypeStruct((peers, 256), F32),
        compiler_params=pltpu.CompilerParams(vmem_limit_bytes=SMALL_BYTES),
    )(owner, hidden, weight, returned)


def arrive_kernel(scale, arrived_ref, parents_ref, total_ref):
    peers = arrived_ref.shape[0]
    slots = parents_ref.shape[1]
    place = one_hot((iota((peers, slots), 1) >> 2) == iota((peers, slots), 0))
    spread = dot(arrived_ref[:, :128].astype(BF16), place, (0, 0))
    keep = (iota(spread.shape, 1) & 3) == (iota(spread.shape, 0) >> 5)
    spread = jnp.where(keep, spread, 0.0)
    parents = spread[:32] + spread[32:64] + spread[64:96] + spread[96:]
    parents_ref[...] = parents.astype(BF16)
    total = jnp.sum(arrived_ref[:, 128:], axis=0, keepdims=True) * scale
    total = jnp.concatenate([total[:, :64], total[:, 64:]], axis=0)
    total_ref[...] = jnp.broadcast_to(total[None], total_ref.shape)


def arrive(arrived, scale, slots):
    peers = arrived.shape[0]
    return pl.pallas_call(
        functools.partial(arrive_kernel, scale),
        name="arrive",
        out_shape=(
            jax.ShapeDtypeStruct((32, slots), BF16),
            jax.ShapeDtypeStruct((peers, 2, 64), F32),
        ),
        compiler_params=pltpu.CompilerParams(vmem_limit_bytes=SMALL_BYTES),
    )(arrived)


def exchange(array, axis):
    return lax.all_to_all(array, axis, 0, 0, tiled=True)


def per_device(features, neighbours, child_count, dest, conv_weight, merge_weight, parent_grad):
    chans, high, low = lax.axis_size("chan"), lax.axis_size("high"), lax.axis_size("low")
    peers = high * low
    width, rows = features.shape
    slots = parent_grad.shape[1]
    channel = lax.axis_index("chan")
    place = jnp.stack([channel, child_count[0]]).astype(jnp.int32)

    cut = cut_to_owners(parent_grad, peers).reshape(high, low, 128)
    halfway = exchange(cut, "high")
    returned = exchange(halfway.swapaxes(0, 1), "low").swapaxes(0, 1).reshape(peers, 128)

    edge = jnp.where(channel == 0, features[:, rows - HALO :], features[:, :HALO])
    pairs = [(p * chans, (p + 1) * chans) for p in range(peers - 1)]
    pairs += [((p + 1) * chans + chans - 1, p * chans + chans - 1) for p in range(peers - 1)]
    halo = lax.ppermute(edge, (*LEAF, "chan"), pairs)

    weight = jnp.swapaxes(conv_weight, 1, 2)
    weights = [weight]
    for shift in range(1, chans):
        ring = [(c, (c + shift) % chans) for c in range(chans)]
        weights.append(lax.ppermute(weight, "chan", ring))

    owner = jnp.where(dest >= 0, dest // slots, -1)
    owner = owner.reshape(slots // 32, 8, 4).transpose(0, 2, 1).reshape(1, slots)
    merge_all = jnp.tile(merge_weight.reshape(KIDS * width, 32), (1, 4))

    hidden = exchange(conv(place, features, halo, neighbours, weights), "chan")
    outbox = merge(owner, hidden, merge_all, returned, peers)
    parents, total = arrive(exchange(outbox, LEAF), 1.0 / math.sqrt(rows), slots)
    grad = exchange(total, LEAF)
    grad = grad.reshape(KIDS // 2, 32, 2, width).swapaxes(1, 2).reshape(KIDS, 32, width)
    return parents, grad.swapaxes(1, 2)


def solution(mesh):
    peers, chans = mesh.devices.shape
    fine = Mesh(mesh.devices.reshape(peers // 16, 16, chans), (*LEAF, "chan"))
    in_specs = (
        P(None, LEAF),
        P(None, LEAF),
        P(LEAF),
        P(LEAF),
        P(None, None, "chan"),
        P(None, None, "chan"),
        P("chan", LEAF),
    )
    out_specs = (P("chan", LEAF), P(None, None, "chan"))
    return jax.shard_map(
        per_device, mesh=fine, in_specs=in_specs, out_specs=out_specs, check_vma=False
    )
```

```python
import functools
import math

import jax
import jax.numpy as jnp
from jax import lax
from jax.experimental import pallas as pl
from jax.experimental.pallas import tpu as pltpu
from jax.sharding import PartitionSpec as P

KIDS = 8
HALO = 1024
BLOCK = 256
VMEM_BYTES = 24 << 20
SMALL_BYTES = 8 << 20
LARGE_BYTES = 56 << 20

BF16 = jnp.bfloat16
F32 = jnp.float32


def dot(a, b, contract):
    return lax.dot_general(a, b, ((contract[:1], contract[1:]), ((), ())), preferred_element_type=F32)


def iota(shape, dim):
    return lax.broadcasted_iota(jnp.int32, shape, dim)


def one_hot(hit):
    return jnp.where(hit, 1.0, 0.0).astype(BF16)


def conv_kernel(
    count_ref,
    features_ref,
    halo_ref,
    offsets_ref,
    weights_ref,
    out_ref,
    nearby,
    arrival,
    window,
    weight,
    gathered,
    swap,
    piece,
):
    channel, valid_rows = lax.axis_index("chan"), count_ref[0]
    width = features_ref.shape[0]
    taps = offsets_ref.shape[0]
    chans = features_ref.shape[1] // HALO
    halo_pieces = HALO // BLOCK
    pieces = window.shape[0] // width
    reach = (2 * HALO) // BLOCK + 1
    mine_at = pl.ds(pl.multiple_of(channel * HALO, HALO), HALO)
    copy = pltpu.make_async_copy(offsets_ref.at[:, mine_at], nearby, arrival)
    copy.start()

    for i in range(pieces):
        at = channel * halo_pieces + i - halo_pieces
        last = features_ref.shape[1] // BLOCK - 1
        inside = jnp.clip(at, 0, last) * BLOCK
        own = features_ref[:, pl.ds(pl.multiple_of(inside, BLOCK), BLOCK)]
        other = halo_ref[:, (i % halo_pieces) * BLOCK : (i % halo_pieces + 1) * BLOCK]
        outside = (at < 0) | (at > last)
        window[i * width : (i + 1) * width, :] = jnp.where(outside, other, own)
    half, part = (taps + 1) // 2, width // chans
    for source in range(chans):
        for tap in range(taps):
            rows = slice(tap % half * part, (tap % half + 1) * part)
            value = weights_ref[source, rows, tap // half * width : (tap // half + 1) * width]
            weight[source * part : (source + 1) * part, tap * width : (tap + 1) * width] = value
    row, lane = iota((BLOCK, BLOCK), 0), iota((BLOCK, BLOCK), 1)
    kid, slot, group = row & 7, (row >> 3) & 3, row >> 5
    swap[...] = one_hot(lane == kid * 32 + slot * 8 + group)

    copy.wait()

    middle = taps // 2
    counted = lax.broadcasted_iota(jnp.int16, (BLOCK, BLOCK), 0)
    one, zero = jnp.ones((BLOCK, BLOCK), BF16), jnp.zeros((BLOCK, BLOCK), BF16)
    steps = HALO // BLOCK

    def gather(step, tap, low, high):
        slot, rows = step % 2, slice(tap * width, (tap + 1) * width)
        if tap == middle:
            centre = (step + halo_pieces) * width
            gathered[slot, rows, :] = window[centre : centre + width, :]
            return
        hit = jnp.where(counted == low[tap : tap + 1, :].astype(jnp.int16), one, zero)
        found = dot(window[step * width : (step + reach) * width, :], hit, (1, 0))
        block = high[tap : tap + 1, :]
        total = found[:width]
        for k in range(1, reach):
            total = jnp.where(block == k, found[k * width : (k + 1) * width], total)
        gathered[slot, rows, :] = total.astype(BF16)

    def activate(step):
        pre_act = dot(weight[...], gathered[step % 2], (1, 0))
        row = channel * HALO + step * BLOCK + iota((1, BLOCK), 1)
        return jnp.where(row < valid_rows, jnp.maximum(pre_act, 0.0), 0.0).astype(BF16)

    def spread_out(step, hidden):
        spread = dot(hidden, swap[...], (1, 0))
        mine = (iota((width, 128), 1) >> 5) == step
        for kid in range(KIDS):
            half = spread[:, (kid // 4) * 128 : (kid // 4 + 1) * 128]
            moved = pltpu.roll(half, (32 * step + 128 - 32 * (kid % 4)) % 128, axis=1)
            rows = slice(kid * width, (kid + 1) * width)
            piece[rows, :] = jnp.where(mine, moved, piece[rows, :])

    hidden = None
    for step in range(steps):
        offsets = nearby[:, step * BLOCK : (step + 1) * BLOCK]
        at = offsets + iota(offsets.shape, 1)
        low = jnp.where(offsets >= 0, at & (BLOCK - 1), -1)
        high = at >> 8
        for tap in range(taps):
            gather(step, tap, low, high)
            if step > 0 and tap == 2:
                hidden = activate(step - 1)
            if step > 0 and tap == 5:
                spread_out(step - 1, hidden)
    spread_out(steps - 1, activate(steps - 1))
    for peer in range(out_ref.shape[0]):
        out_ref[peer] = piece[...].astype(BF16)


def conv(count, features, halo, offsets, weights):
    width = features.shape[0]
    taps = offsets.shape[0]
    vmem = pl.BlockSpec(memory_space=pltpu.VMEM)
    return pl.pallas_call(
        conv_kernel,
        name="conv",
        out_shape=jax.ShapeDtypeStruct((weights.shape[0], KIDS * width, HALO // KIDS), BF16),
        in_specs=[
            pl.BlockSpec(memory_space=pltpu.SMEM),
            vmem,
            vmem,
            pl.BlockSpec(memory_space=pltpu.HBM),
            vmem,
        ],
        out_specs=vmem,
        scratch_shapes=[
            pltpu.VMEM((taps, HALO), jnp.int32),
            pltpu.SemaphoreType.DMA,
            pltpu.VMEM((3 * HALO // BLOCK * width, BLOCK), BF16),
            pltpu.VMEM((width, taps * width), BF16),
            pltpu.VMEM((2, taps * width, BLOCK), BF16),
            pltpu.VMEM((BLOCK, BLOCK), BF16),
            pltpu.VMEM((KIDS * width, HALO // KIDS), F32),
        ],
        compiler_params=pltpu.CompilerParams(vmem_limit_bytes=VMEM_BYTES),
        cost_estimate=pl.CostEstimate(flops=8_000_000_000, bytes_accessed=2_000_000, transcendentals=0),
    )(count, features, halo, offsets, weights)


def pack_kernel(weight_hbm, out_ref, weight_ref, arrival):
    copy = pltpu.make_async_copy(weight_hbm, weight_ref, arrival)
    copy.start()
    taps, part, width = weight_ref.shape
    half = (taps + 1) // 2
    out_ref[0, (half - 1) * part :, width:] = jnp.zeros((part, width), BF16)
    copy.wait()
    for tap in range(taps):
        rows = slice(tap % half * part, (tap % half + 1) * part)
        out_ref[0, rows, tap // half * width : (tap // half + 1) * width] = weight_ref[tap]
    packed = out_ref[0]
    for peer in range(1, out_ref.shape[0]):
        out_ref[peer] = packed


def pack(weight, chans):
    taps, part, width = weight.shape
    return pl.pallas_call(
        pack_kernel,
        name="pack",
        out_shape=jax.ShapeDtypeStruct((chans, (taps + 1) // 2 * part, 2 * width), BF16),
        in_specs=[pl.BlockSpec(memory_space=pl.ANY)],
        scratch_shapes=[pltpu.VMEM(weight.shape, BF16), pltpu.SemaphoreType.DMA],
        compiler_params=pltpu.CompilerParams(vmem_limit_bytes=LARGE_BYTES),
    )(weight)


def cut_kernel(features_hbm, grad_hbm, edge_ref, cut_ref, grad_ref, edge_arrival, grad_arrival):
    peers, slots = cut_ref.shape[0], grad_ref.shape[1]
    last = features_hbm.shape[1] - HALO
    start = pl.multiple_of(jnp.where(lax.axis_index("chan") == 0, last, 0), HALO)
    edge_copy = pltpu.make_async_copy(features_hbm.at[:, pl.ds(start, HALO)], edge_ref, edge_arrival)
    grad_copy = pltpu.make_async_copy(grad_hbm, grad_ref, grad_arrival)
    edge_copy.start()
    grad_copy.start()
    where = one_hot((iota((peers, slots), 1) >> 2) == iota((peers, slots), 0))
    grad_copy.wait()
    grad = jnp.concatenate([grad_ref[...]] * 4, axis=0).astype(F32)
    keep = (iota(grad.shape, 1) & 3) == (iota(grad.shape, 0) >> 5)
    grad = jnp.where(keep, grad, 0.0).astype(BF16)
    cut_ref[...] = dot(where, grad, (1, 1))
    edge_copy.wait()


def cut(features, parent_grad, peers):
    hbm = pl.BlockSpec(memory_space=pl.ANY)
    return pl.pallas_call(
        cut_kernel,
        name="cut",
        out_shape=(
            jax.ShapeDtypeStruct((features.shape[0], HALO), BF16),
            jax.ShapeDtypeStruct((peers, 128), F32),
        ),
        in_specs=[hbm, hbm],
        scratch_shapes=[
            pltpu.VMEM(parent_grad.shape, BF16),
            pltpu.SemaphoreType.DMA,
            pltpu.SemaphoreType.DMA,
        ],
        compiler_params=pltpu.CompilerParams(vmem_limit_bytes=LARGE_BYTES),
    )(features, parent_grad)


def merge_kernel(owner_ref, hidden_ref, weight_ref, returned_ref, out_ref):
    peers = out_ref.shape[0]
    count = hidden_ref.shape[0]
    slots = owner_ref.shape[1]
    share = slots // count
    depth = hidden_ref.shape[1]
    place = one_hot(iota((peers, slots), 0) == owner_ref[...])
    own = ((iota((slots, 128), 0) >> 3) & 3) == (iota((slots, 128), 1) >> 5)
    fetched = jnp.where(own, dot(place, returned_ref[...].astype(BF16), (0, 0)), 0.0)
    fetched = fetched + pltpu.roll(fetched, 64, axis=1)
    fetched = fetched + pltpu.roll(fetched, 32, axis=1)
    fetched = fetched.astype(BF16)
    outbox = jnp.zeros((peers, 128), F32)
    grad = jnp.zeros((128, depth), F32)
    for piece in range(count):
        hidden = hidden_ref[piece]
        rows = slice(piece * share, (piece + 1) * share)
        merged = dot(hidden, weight_ref[...], (0, 0))
        merged = jnp.where(own[rows], merged, 0.0).astype(BF16)
        outbox = outbox + dot(place[:, rows], merged, (1, 0))
        grad = grad + dot(fetched[rows], hidden, (0, 1))
    out_ref[:, :128] = outbox
    for k in range(depth // 128):
        out_ref[k * 32 : (k + 1) * 32, 128:] = grad[:32, k * 128 : (k + 1) * 128]


def merge(owner, hidden, weight, returned, peers):
    return pl.pallas_call(
        merge_kernel,
        name="merge",
        out_shape=jax.ShapeDtypeStruct((peers, 256), F32),
        compiler_params=pltpu.CompilerParams(vmem_limit_bytes=SMALL_BYTES),
    )(owner, hidden, weight, returned)


def arrive_kernel(scale, arrived_ref, parents_ref, total_ref):
    peers = arrived_ref.shape[0]
    slots = parents_ref.shape[1]
    place = one_hot((iota((peers, slots), 1) >> 2) == iota((peers, slots), 0))
    spread = dot(arrived_ref[:, :128].astype(BF16), place, (0, 0))
    keep = (iota(spread.shape, 1) & 3) == (iota(spread.shape, 0) >> 5)
    spread = jnp.where(keep, spread, 0.0)
    parents = spread[:32] + spread[32:64] + spread[64:96] + spread[96:]
    parents_ref[...] = parents.astype(BF16)
    total = jnp.sum(arrived_ref[:, 128:], axis=0, keepdims=True) * scale
    total_ref[...] = jnp.broadcast_to(total, total_ref.shape)


def arrive(arrived, scale, slots):
    peers = arrived.shape[0]
    return pl.pallas_call(
        functools.partial(arrive_kernel, scale),
        name="arrive",
        out_shape=(
            jax.ShapeDtypeStruct((32, slots), BF16),
            jax.ShapeDtypeStruct((peers, 128), F32),
        ),
        compiler_params=pltpu.CompilerParams(vmem_limit_bytes=SMALL_BYTES),
    )(arrived)


def finish_kernel(total_ref, out_ref):
    kids, outs, width = out_ref.shape
    for kid in range(kids):
        rows = slice(kid // 2 * outs, (kid // 2 + 1) * outs)
        out_ref[kid] = total_ref[rows, kid % 2 * width : (kid % 2 + 1) * width]


def finish(total, width):
    return pl.pallas_call(
        finish_kernel,
        name="finish",
        out_shape=jax.ShapeDtypeStruct((KIDS, 32, width), F32),
        compiler_params=pltpu.CompilerParams(vmem_limit_bytes=SMALL_BYTES),
    )(total)


def exchange(array, axis):
    return lax.all_to_all(array, axis, 0, 0, tiled=True)


def per_device(features, neighbours, child_count, dest, conv_weight, merge_weight, parent_grad):
    chans, peers = lax.axis_size("chan"), lax.axis_size("leaf")
    width, rows = features.shape
    slots = parent_grad.shape[1]
    weights = exchange(pack(jnp.swapaxes(conv_weight, 1, 2), chans), "chan")
    edge, grad_out = cut(features, parent_grad, peers)
    pairs = [(p * chans, (p + 1) * chans) for p in range(peers - 1)]
    pairs += [((p + 1) * chans + chans - 1, p * chans + chans - 1) for p in range(peers - 1)]
    halo = lax.ppermute(edge, ("leaf", "chan"), pairs)
    weights, grad_out = lax.optimization_barrier((weights, grad_out))
    returned = exchange(grad_out, "leaf")

    owner = jnp.where(dest >= 0, dest // slots, -1)
    owner = owner.reshape(slots // 32, 8, 4).transpose(0, 2, 1).reshape(1, slots)
    merge_all = jnp.tile(merge_weight.reshape(KIDS * width, 32), (1, 4))

    hidden = exchange(conv(child_count, features, halo, neighbours, weights), "chan")
    outbox = merge(owner, hidden, merge_all, returned, peers)
    parents, total = arrive(exchange(outbox, "leaf"), 1.0 / math.sqrt(rows), slots)
    grad = finish(exchange(total, "leaf"), width)
    return parents, grad.swapaxes(1, 2)


def solution(mesh):
    in_specs = (
        P(None, "leaf"),
        P(None, "leaf"),
        P("leaf"),
        P("leaf"),
        P(None, None, "chan"),
        P(None, None, "chan"),
        P("chan", "leaf"),
    )
    out_specs = (P("chan", "leaf"), P(None, None, "chan"))
    return jax.shard_map(
        per_device, mesh=mesh, in_specs=in_specs, out_specs=out_specs, check_vma=False
    )
```

```python
import functools
import math

import jax
import jax.numpy as jnp
from jax import lax
from jax.experimental import pallas as pl
from jax.experimental.pallas import tpu as pltpu
from jax.sharding import PartitionSpec as P

KIDS = 8
HALO = 1024
BLOCK = 256
VMEM_BYTES = 24 << 20
SMALL_BYTES = 8 << 20
LARGE_BYTES = 56 << 20

BF16 = jnp.bfloat16
F32 = jnp.float32


def dot(a, b, contract):
    return lax.dot_general(a, b, ((contract[:1], contract[1:]), ((), ())), preferred_element_type=F32)


def iota(shape, dim):
    return lax.broadcasted_iota(jnp.int32, shape, dim)


def one_hot(hit):
    return jnp.where(hit, 1.0, 0.0).astype(BF16)


def conv_kernel(
    count_ref,
    features_ref,
    halo_ref,
    offsets_ref,
    weights_ref,
    out_ref,
    nearby,
    arrival,
    window,
    weight,
    gathered,
    swap,
):
    channel, valid_rows = lax.axis_index("chan"), count_ref[0]
    width = features_ref.shape[0]
    taps = offsets_ref.shape[0]
    chans = features_ref.shape[1] // HALO
    halo_pieces = HALO // BLOCK
    pieces = window.shape[0] // width
    reach = (2 * HALO) // BLOCK + 1
    mine_at = pl.ds(pl.multiple_of(channel * HALO, HALO), HALO)
    copy = pltpu.make_async_copy(offsets_ref.at[:, mine_at], nearby, arrival)
    copy.start()

    for i in range(pieces):
        at = channel * halo_pieces + i - halo_pieces
        last = features_ref.shape[1] // BLOCK - 1
        inside = jnp.clip(at, 0, last) * BLOCK
        own = features_ref[:, pl.ds(pl.multiple_of(inside, BLOCK), BLOCK)]
        other = halo_ref[:, (i % halo_pieces) * BLOCK : (i % halo_pieces + 1) * BLOCK]
        outside = (at < 0) | (at > last)
        window[i * width : (i + 1) * width, :] = jnp.where(outside, other, own)
    half, part = (taps + 1) // 2, width // chans
    for source in range(chans):
        for tap in range(taps):
            rows = slice(tap % half * part, (tap % half + 1) * part)
            value = weights_ref[source, rows, tap // half * width : (tap // half + 1) * width]
            weight[source * part : (source + 1) * part, tap * width : (tap + 1) * width] = value
    row, lane = iota((BLOCK, BLOCK), 0), iota((BLOCK, BLOCK), 1)
    kid, slot, group = row & 7, (row >> 3) & 3, row >> 5
    swap[...] = one_hot(lane == kid * 32 + slot * 8 + group)

    copy.wait()

    middle = taps // 2
    counted = lax.broadcasted_iota(jnp.int16, (BLOCK, BLOCK), 0)
    one, zero = jnp.ones((BLOCK, BLOCK), BF16), jnp.zeros((BLOCK, BLOCK), BF16)
    steps = HALO // BLOCK

    def gather(step, tap, low, high):
        slot, rows = step % 2, slice(tap * width, (tap + 1) * width)
        if tap == middle:
            centre = (step + halo_pieces) * width
            gathered[slot, rows, :] = window[centre : centre + width, :]
            return
        hit = jnp.where(counted == low[tap : tap + 1, :].astype(jnp.int16), one, zero)
        found = dot(window[step * width : (step + reach) * width, :], hit, (1, 0))
        block = high[tap : tap + 1, :]
        total = found[:width]
        for k in range(1, reach):
            total = jnp.where(block == k, found[k * width : (k + 1) * width], total)
        gathered[slot, rows, :] = total.astype(BF16)

    def activate(step):
        pre_act = dot(weight[...], gathered[step % 2], (1, 0))
        row = channel * HALO + step * BLOCK + iota((1, BLOCK), 1)
        return jnp.where(row < valid_rows, jnp.maximum(pre_act, 0.0), 0.0).astype(BF16)

    hidden = []
    for step in range(steps):
        offsets = nearby[:, step * BLOCK : (step + 1) * BLOCK]
        at = offsets + iota(offsets.shape, 1)
        low = jnp.where(offsets >= 0, at & (BLOCK - 1), -1)
        high = at >> 8
        for tap in range(taps):
            gather(step, tap, low, high)
            if step > 0 and tap == 2:
                hidden.append(activate(step - 1))
    hidden.append(activate(steps - 1))
    spread = dot(jnp.concatenate(hidden, axis=0), swap[...], (1, 0))
    group = iota((width, 128), 1) >> 5
    for kid in range(KIDS):
        total = None
        for step in range(steps):
            half = spread[step * width : (step + 1) * width, kid // 4 * 128 : (kid // 4 + 1) * 128]
            shift = (32 * step + 128 - 32 * (kid % 4)) % 128
            moved = pltpu.roll(half, shift, axis=1) if shift else half
            total = moved if total is None else jnp.where(group == step, moved, total)
        rows = slice(kid * width, (kid + 1) * width)
        for peer in range(out_ref.shape[0]):
            out_ref[peer, rows, :] = total.astype(BF16)


def conv(count, features, halo, offsets, weights):
    width = features.shape[0]
    taps = offsets.shape[0]
    vmem = pl.BlockSpec(memory_space=pltpu.VMEM)
    return pl.pallas_call(
        conv_kernel,
        name="conv",
        out_shape=jax.ShapeDtypeStruct((weights.shape[0], KIDS * width, HALO // KIDS), BF16),
        in_specs=[
            pl.BlockSpec(memory_space=pltpu.SMEM),
            vmem,
            vmem,
            pl.BlockSpec(memory_space=pltpu.HBM),
            vmem,
        ],
        out_specs=vmem,
        scratch_shapes=[
            pltpu.VMEM((taps, HALO), jnp.int32),
            pltpu.SemaphoreType.DMA,
            pltpu.VMEM((3 * HALO // BLOCK * width, BLOCK), BF16),
            pltpu.VMEM((width, taps * width), BF16),
            pltpu.VMEM((2, taps * width, BLOCK), BF16),
            pltpu.VMEM((BLOCK, BLOCK), BF16),
        ],
        compiler_params=pltpu.CompilerParams(vmem_limit_bytes=VMEM_BYTES),
        cost_estimate=pl.CostEstimate(flops=8_000_000_000, bytes_accessed=2_000_000, transcendentals=0),
    )(count, features, halo, offsets, weights)


def pack_kernel(weight_hbm, out_ref, weight_ref, arrival):
    copy = pltpu.make_async_copy(weight_hbm, weight_ref, arrival)
    copy.start()
    taps, part, width = weight_ref.shape
    half = (taps + 1) // 2
    out_ref[0, (half - 1) * part :, width:] = jnp.zeros((part, width), BF16)
    copy.wait()
    for tap in range(taps):
        rows = slice(tap % half * part, (tap % half + 1) * part)
        out_ref[0, rows, tap // half * width : (tap // half + 1) * width] = weight_ref[tap]
    packed = out_ref[0]
    for peer in range(1, out_ref.shape[0]):
        out_ref[peer] = packed


def pack(weight, chans):
    taps, part, width = weight.shape
    return pl.pallas_call(
        pack_kernel,
        name="pack",
        out_shape=jax.ShapeDtypeStruct((chans, (taps + 1) // 2 * part, 2 * width), BF16),
        in_specs=[pl.BlockSpec(memory_space=pl.ANY)],
        scratch_shapes=[pltpu.VMEM(weight.shape, BF16), pltpu.SemaphoreType.DMA],
        compiler_params=pltpu.CompilerParams(vmem_limit_bytes=LARGE_BYTES),
    )(weight)


def cut_kernel(features_hbm, grad_hbm, edge_ref, cut_ref, grad_ref, edge_arrival, grad_arrival):
    peers, slots = cut_ref.shape[0], grad_ref.shape[1]
    last = features_hbm.shape[1] - HALO
    start = pl.multiple_of(jnp.where(lax.axis_index("chan") == 0, last, 0), HALO)
    edge_copy = pltpu.make_async_copy(features_hbm.at[:, pl.ds(start, HALO)], edge_ref, edge_arrival)
    grad_copy = pltpu.make_async_copy(grad_hbm, grad_ref, grad_arrival)
    edge_copy.start()
    grad_copy.start()
    where = one_hot((iota((peers, slots), 1) >> 2) == iota((peers, slots), 0))
    grad_copy.wait()
    grad = jnp.concatenate([grad_ref[...]] * 4, axis=0).astype(F32)
    keep = (iota(grad.shape, 1) & 3) == (iota(grad.shape, 0) >> 5)
    grad = jnp.where(keep, grad, 0.0).astype(BF16)
    cut_ref[...] = dot(where, grad, (1, 1))
    edge_copy.wait()


def cut(features, parent_grad, peers):
    hbm = pl.BlockSpec(memory_space=pl.ANY)
    return pl.pallas_call(
        cut_kernel,
        name="cut",
        out_shape=(
            jax.ShapeDtypeStruct((features.shape[0], HALO), BF16),
            jax.ShapeDtypeStruct((peers, 128), F32),
        ),
        in_specs=[hbm, hbm],
        scratch_shapes=[
            pltpu.VMEM(parent_grad.shape, BF16),
            pltpu.SemaphoreType.DMA,
            pltpu.SemaphoreType.DMA,
        ],
        compiler_params=pltpu.CompilerParams(vmem_limit_bytes=LARGE_BYTES),
    )(features, parent_grad)


def fetch_kernel(owner_ref, returned_ref, place_ref, fetched_ref):
    place = one_hot(iota(place_ref.shape, 0) == owner_ref[...])
    place_ref[...] = place
    fetched = dot(place, returned_ref[...].astype(BF16), (0, 0))
    own = ((iota(fetched.shape, 0) >> 3) & 3) == (iota(fetched.shape, 1) >> 5)
    fetched = jnp.where(own, fetched, 0.0)
    fetched = fetched + pltpu.roll(fetched, 64, axis=1)
    fetched = fetched + pltpu.roll(fetched, 32, axis=1)
    fetched_ref[...] = fetched.astype(BF16)


def fetch(owner, returned):
    peers, slots = returned.shape[0], owner.shape[1]
    return pl.pallas_call(
        fetch_kernel,
        name="fetch",
        out_shape=(
            jax.ShapeDtypeStruct((peers, slots), BF16),
            jax.ShapeDtypeStruct((slots, 128), BF16),
        ),
        compiler_params=pltpu.CompilerParams(vmem_limit_bytes=SMALL_BYTES),
    )(owner, returned)


def merge_kernel(place_ref, fetched_ref, hidden_ref, weight_ref, out_ref):
    peers, slots = place_ref.shape
    count, depth = hidden_ref.shape[:2]
    share = slots // count
    own = ((iota((share, 128), 0) >> 3) & 3) == (iota((share, 128), 1) >> 5)
    outbox = jnp.zeros((peers, 128), F32)
    grad = jnp.zeros((128, depth), F32)
    for piece in range(count):
        hidden = hidden_ref[piece]
        rows = slice(piece * share, (piece + 1) * share)
        merged = dot(hidden, weight_ref[...], (0, 0))
        merged = jnp.where(own, merged, 0.0).astype(BF16)
        outbox = outbox + dot(place_ref[:, rows], merged, (1, 0))
        grad = grad + dot(fetched_ref[rows, :], hidden, (0, 1))
    out_ref[pl.ds(0, peers, stride=2), :] = outbox
    for k in range(depth // 128):
        out_ref[pl.ds(64 * k + 1, 32, stride=2), :] = grad[:32, k * 128 : (k + 1) * 128]


def merge(place, fetched, hidden, weight):
    return pl.pallas_call(
        merge_kernel,
        name="merge",
        out_shape=jax.ShapeDtypeStruct((2 * place.shape[0], 128), F32),
        compiler_params=pltpu.CompilerParams(vmem_limit_bytes=SMALL_BYTES),
    )(place, fetched, hidden, weight)


def arrive_kernel(scale, arrived_ref, parents_ref, total_ref):
    peers = total_ref.shape[0]
    slots = parents_ref.shape[1]
    place = one_hot((iota((peers, slots), 1) >> 2) == iota((peers, slots), 0))
    spread = dot(arrived_ref[pl.ds(0, peers, stride=2), :].astype(BF16), place, (0, 0))
    keep = (iota(spread.shape, 1) & 3) == (iota(spread.shape, 0) >> 5)
    spread = jnp.where(keep, spread, 0.0)
    parents = spread[:32] + spread[32:64] + spread[64:96] + spread[96:]
    parents_ref[...] = parents.astype(BF16)
    total = jnp.sum(arrived_ref[pl.ds(1, peers, stride=2), :], axis=0, keepdims=True) * scale
    total_ref[...] = jnp.broadcast_to(total, total_ref.shape)


def arrive(arrived, scale, slots):
    peers = arrived.shape[0] // 2
    return pl.pallas_call(
        functools.partial(arrive_kernel, scale),
        name="arrive",
        out_shape=(
            jax.ShapeDtypeStruct((32, slots), BF16),
            jax.ShapeDtypeStruct((peers, 128), F32),
        ),
        compiler_params=pltpu.CompilerParams(vmem_limit_bytes=SMALL_BYTES),
    )(arrived)


def finish_kernel(total_ref, out_ref):
    kids, outs, width = out_ref.shape
    for kid in range(kids):
        rows = slice(kid // 2 * outs, (kid // 2 + 1) * outs)
        out_ref[kid] = total_ref[rows, kid % 2 * width : (kid % 2 + 1) * width]


def finish(total, width):
    return pl.pallas_call(
        finish_kernel,
        name="finish",
        out_shape=jax.ShapeDtypeStruct((KIDS, 32, width), F32),
        compiler_params=pltpu.CompilerParams(vmem_limit_bytes=SMALL_BYTES),
    )(total)


def exchange(array, axis):
    return lax.all_to_all(array, axis, 0, 0, tiled=True)


def per_device(features, neighbours, child_count, dest, conv_weight, merge_weight, parent_grad):
    chans, peers = lax.axis_size("chan"), lax.axis_size("leaf")
    width, rows = features.shape
    slots = parent_grad.shape[1]
    weights = exchange(pack(jnp.swapaxes(conv_weight, 1, 2), chans), "chan")
    edge, grad_out = cut(features, parent_grad, peers)
    pairs = [(p * chans, (p + 1) * chans) for p in range(peers - 1)]
    pairs += [((p + 1) * chans + chans - 1, p * chans + chans - 1) for p in range(peers - 1)]
    halo = lax.ppermute(edge, ("leaf", "chan"), pairs)
    weights, grad_out = lax.optimization_barrier((weights, grad_out))
    returned = exchange(grad_out, "leaf")

    owner = jnp.where(dest >= 0, dest // slots, -1)
    owner = owner.reshape(slots // 32, 8, 4).transpose(0, 2, 1).reshape(1, slots)
    merge_all = jnp.tile(merge_weight.reshape(KIDS * width, 32), (1, 4))

    hidden = exchange(conv(child_count, features, halo, neighbours, weights), "chan")
    outbox = merge(*fetch(owner, returned), hidden, merge_all).reshape(peers, 2, 128)
    arrived = exchange(outbox, "leaf").reshape(2 * peers, 128)
    parents, total = arrive(arrived, 1.0 / math.sqrt(rows), slots)
    grad = finish(exchange(total, "leaf"), width)
    return parents, grad.swapaxes(1, 2)


def solution(mesh):
    in_specs = (
        P(None, "leaf"),
        P(None, "leaf"),
        P("leaf"),
        P("leaf"),
        P(None, None, "chan"),
        P(None, None, "chan"),
        P("chan", "leaf"),
    )
    out_specs = (P("chan", "leaf"), P(None, None, "chan"))
    return jax.shard_map(
        per_device, mesh=mesh, in_specs=in_specs, out_specs=out_specs, check_vma=False
    )
```

```python
import functools
import math

import jax
import jax.numpy as jnp
from jax import lax
from jax.experimental import pallas as pl
from jax.experimental.pallas import tpu as pltpu
from jax.sharding import PartitionSpec as P

KIDS = 8
HALO = 1024
BLOCK = 256
VMEM_BYTES = 24 << 20
SMALL_BYTES = 8 << 20
LARGE_BYTES = 56 << 20

BF16 = jnp.bfloat16
F32 = jnp.float32


def dot(a, b, contract):
    return lax.dot_general(a, b, ((contract[:1], contract[1:]), ((), ())), preferred_element_type=F32)


def iota(shape, dim):
    return lax.broadcasted_iota(jnp.int32, shape, dim)


def one_hot(hit):
    return jnp.where(hit, 1.0, 0.0).astype(BF16)


def conv_kernel(
    count_ref,
    features_ref,
    halo_ref,
    offsets_ref,
    weights_ref,
    out_ref,
    window,
    weight,
    gathered,
    swap,
):
    channel, valid_rows = lax.axis_index("chan"), count_ref[0]
    width = features_ref.shape[0]
    taps = offsets_ref.shape[0]
    chans = features_ref.shape[1] // HALO
    halo_pieces = HALO // BLOCK
    pieces = window.shape[0] // width
    reach = (2 * HALO) // BLOCK + 1

    for i in range(pieces):
        at = channel * halo_pieces + i - halo_pieces
        last = features_ref.shape[1] // BLOCK - 1
        inside = jnp.clip(at, 0, last) * BLOCK
        own = features_ref[:, pl.ds(pl.multiple_of(inside, BLOCK), BLOCK)]
        other = halo_ref[:, (i % halo_pieces) * BLOCK : (i % halo_pieces + 1) * BLOCK]
        outside = (at < 0) | (at > last)
        window[i * width : (i + 1) * width, :] = jnp.where(outside, other, own)
    half, part = (taps + 1) // 2, width // chans
    for source in range(chans):
        for tap in range(taps):
            rows = slice(tap % half * part, (tap % half + 1) * part)
            value = weights_ref[(source - first_of(chans)) % chans, rows, tap // half * width : (tap // half + 1) * width]
            weight[source * part : (source + 1) * part, tap * width : (tap + 1) * width] = value
    row, lane = iota((BLOCK, BLOCK), 0), iota((BLOCK, BLOCK), 1)
    kid, slot, group = row & 7, (row >> 3) & 3, row >> 5
    swap[...] = one_hot(lane == kid * 32 + slot * 8 + group)

    middle = taps // 2
    counted = lax.broadcasted_iota(jnp.int16, (BLOCK, BLOCK), 0)
    one, zero = jnp.ones((BLOCK, BLOCK), BF16), jnp.zeros((BLOCK, BLOCK), BF16)
    steps = HALO // BLOCK

    def gather(step, tap, low, high):
        slot, rows = step % 2, slice(tap * width, (tap + 1) * width)
        if tap == middle:
            centre = (step + halo_pieces) * width
            gathered[slot, rows, :] = window[centre : centre + width, :]
            return
        hit = jnp.where(counted == low[tap : tap + 1, :].astype(jnp.int16), one, zero)
        found = dot(window[step * width : (step + reach) * width, :], hit, (1, 0))
        block = high[tap : tap + 1, :]
        total = found[:width]
        for k in range(1, reach):
            total = jnp.where(block == k, found[k * width : (k + 1) * width], total)
        gathered[slot, rows, :] = total.astype(BF16)

    def activate(step):
        pre_act = dot(weight[...], gathered[step % 2], (1, 0))
        row = channel * HALO + step * BLOCK + iota((1, BLOCK), 1)
        return jnp.where(row < valid_rows, jnp.maximum(pre_act, 0.0), 0.0).astype(BF16)

    hidden = []
    for step in range(steps):
        start = pl.multiple_of(channel * HALO + step * BLOCK, BLOCK)
        offsets = offsets_ref[:, pl.ds(start, BLOCK)]
        at = offsets + iota(offsets.shape, 1)
        low = jnp.where(offsets >= 0, at & (BLOCK - 1), -1)
        high = at >> 8
        for tap in range(taps):
            gather(step, tap, low, high)
            if step > 0 and tap == 2:
                hidden.append(activate(step - 1))
    hidden.append(activate(steps - 1))
    spread = dot(jnp.concatenate(hidden, axis=0), swap[...], (1, 0))
    group = iota((width, 128), 1) >> 5
    for kid in range(KIDS):
        total = None
        for step in range(steps):
            half = spread[step * width : (step + 1) * width, kid // 4 * 128 : (kid // 4 + 1) * 128]
            shift = (32 * step + 128 - 32 * (kid % 4)) % 128
            moved = pltpu.roll(half, shift, axis=1) if shift else half
            total = moved if total is None else jnp.where(group == step, moved, total)
        rows = slice(kid * width, (kid + 1) * width)
        for peer in range(out_ref.shape[0]):
            out_ref[peer, rows, :] = total.astype(BF16)


def conv(count, features, halo, offsets, weights):
    width = features.shape[0]
    taps = offsets.shape[0]
    vmem = pl.BlockSpec(memory_space=pltpu.VMEM)
    return pl.pallas_call(
        conv_kernel,
        name="conv",
        out_shape=jax.ShapeDtypeStruct((weights.shape[0], KIDS * width, HALO // KIDS), BF16),
        in_specs=[
            pl.BlockSpec(memory_space=pltpu.SMEM),
            vmem,
            vmem,
            vmem,
            vmem,
        ],
        out_specs=vmem,
        scratch_shapes=[
            pltpu.VMEM((3 * HALO // BLOCK * width, BLOCK), BF16),
            pltpu.VMEM((width, taps * width), BF16),
            pltpu.VMEM((2, taps * width, BLOCK), BF16),
            pltpu.VMEM((BLOCK, BLOCK), BF16),
        ],
        compiler_params=pltpu.CompilerParams(vmem_limit_bytes=VMEM_BYTES),
        cost_estimate=pl.CostEstimate(flops=8_000_000_000, bytes_accessed=2_000_000, transcendentals=0),
    )(count, features, halo, offsets, weights)


def pack_kernel(weight_ref, out_ref):
    taps, part, width = weight_ref.shape
    half = (taps + 1) // 2
    out_ref[0, (half - 1) * part :, width:] = jnp.zeros((part, width), BF16)
    for tap in range(taps):
        rows = slice(tap % half * part, (tap % half + 1) * part)
        out_ref[0, rows, tap // half * width : (tap // half + 1) * width] = weight_ref[tap]
    packed = out_ref[0]
    for peer in range(1, out_ref.shape[0]):
        out_ref[peer] = packed


def pack(weight, chans):
    taps, part, width = weight.shape
    return pl.pallas_call(
        pack_kernel,
        name="pack",
        out_shape=jax.ShapeDtypeStruct((chans, (taps + 1) // 2 * part, 2 * width), BF16),
        in_specs=[pl.BlockSpec(memory_space=pltpu.VMEM)],
        out_specs=pl.BlockSpec(memory_space=pltpu.VMEM),
        compiler_params=pltpu.CompilerParams(vmem_limit_bytes=SMALL_BYTES),
    )(weight)


def cut_kernel(features_hbm, grad_hbm, edge_ref, cut_ref, grad_ref, edge_arrival, grad_arrival):
    peers, slots = cut_ref.shape[0], grad_ref.shape[1]
    last = features_hbm.shape[1] - HALO
    start = pl.multiple_of(jnp.where(lax.axis_index("chan") == 0, last, 0), HALO)
    edge_copy = pltpu.make_async_copy(features_hbm.at[:, pl.ds(start, HALO)], edge_ref, edge_arrival)
    grad_copy = pltpu.make_async_copy(grad_hbm, grad_ref, grad_arrival)
    edge_copy.start()
    grad_copy.start()
    peer = lax.rem(iota((peers, slots), 0) + first_of(peers), peers)
    where = one_hot((iota((peers, slots), 1) >> 2) == peer)
    grad_copy.wait()
    grad = jnp.concatenate([grad_ref[...]] * 4, axis=0).astype(F32)
    keep = (iota(grad.shape, 1) & 3) == (iota(grad.shape, 0) >> 5)
    grad = jnp.where(keep, grad, 0.0).astype(BF16)
    cut_ref[...] = dot(where, grad, (1, 1))
    edge_copy.wait()


def cut(features, parent_grad, peers):
    hbm = pl.BlockSpec(memory_space=pl.ANY)
    return pl.pallas_call(
        cut_kernel,
        name="cut",
        out_shape=(
            jax.ShapeDtypeStruct((features.shape[0], HALO), BF16),
            jax.ShapeDtypeStruct((peers, 128), F32),
        ),
        in_specs=[hbm, hbm],
        scratch_shapes=[
            pltpu.VMEM(parent_grad.shape, BF16),
            pltpu.SemaphoreType.DMA,
            pltpu.SemaphoreType.DMA,
        ],
        compiler_params=pltpu.CompilerParams(vmem_limit_bytes=LARGE_BYTES),
    )(features, parent_grad)


def fetch_kernel(owner_ref, returned_ref, place_ref, fetched_ref):
    place = one_hot(iota(place_ref.shape, 0) == owner_ref[...])
    place_ref[...] = place
    fetched = dot(place, returned_ref[...].astype(BF16), (0, 0))
    own = ((iota(fetched.shape, 0) >> 3) & 3) == (iota(fetched.shape, 1) >> 5)
    fetched = jnp.where(own, fetched, 0.0)
    fetched = fetched + pltpu.roll(fetched, 64, axis=1)
    fetched = fetched + pltpu.roll(fetched, 32, axis=1)
    fetched_ref[...] = fetched.astype(BF16)


def fetch(owner, returned):
    peers, slots = returned.shape[0], owner.shape[1]
    return pl.pallas_call(
        fetch_kernel,
        name="fetch",
        out_shape=(
            jax.ShapeDtypeStruct((peers, slots), BF16),
            jax.ShapeDtypeStruct((slots, 128), BF16),
        ),
        compiler_params=pltpu.CompilerParams(vmem_limit_bytes=SMALL_BYTES),
    )(owner, returned)


def merge_kernel(place_ref, fetched_ref, hidden_ref, weight_ref, out_ref):
    peers, slots = place_ref.shape
    count, depth = hidden_ref.shape[:2]
    share = slots // count
    own = ((iota((share, 128), 0) >> 3) & 3) == (iota((share, 128), 1) >> 5)
    outbox = jnp.zeros((peers, 128), F32)
    grad = jnp.zeros((128, depth), F32)
    for piece in range(count):
        hidden = hidden_ref[piece]
        quarter = (piece + first_of(count)) % count
        rows = slice(quarter * share, (quarter + 1) * share)
        merged = dot(hidden, weight_ref[...], (0, 0))
        merged = jnp.where(own, merged, 0.0).astype(BF16)
        outbox = outbox + dot(place_ref[:, rows], merged, (1, 0))
        grad = grad + dot(fetched_ref[rows, :], hidden, (0, 1))
    out_ref[pl.ds(0, peers, stride=2), :] = outbox
    for k in range(depth // 128):
        out_ref[pl.ds(64 * k + 1, 32, stride=2), :] = grad[:32, k * 128 : (k + 1) * 128]


def merge(place, fetched, hidden, weight):
    return pl.pallas_call(
        merge_kernel,
        name="merge",
        out_shape=jax.ShapeDtypeStruct((2 * place.shape[0], 128), F32),
        compiler_params=pltpu.CompilerParams(vmem_limit_bytes=SMALL_BYTES),
    )(place, fetched, hidden, weight)


def total_kernel(scale, arrived_ref, total_ref):
    peers = total_ref.shape[0]
    total = jnp.sum(arrived_ref[pl.ds(1, peers, stride=2), :], axis=0, keepdims=True) * scale
    total_ref[...] = jnp.broadcast_to(total, total_ref.shape)


def total_of(arrived, scale):
    return pl.pallas_call(
        functools.partial(total_kernel, scale),
        name="total",
        out_shape=jax.ShapeDtypeStruct((arrived.shape[0] // 2, 128), F32),
        compiler_params=pltpu.CompilerParams(vmem_limit_bytes=SMALL_BYTES),
    )(arrived)


def parents_kernel(arrived_ref, parents_ref):
    peers, slots = arrived_ref.shape[0] // 2, parents_ref.shape[1]
    peer = lax.rem(iota((peers, slots), 0) + first_of(peers), peers)
    place = one_hot((iota((peers, slots), 1) >> 2) == peer)
    spread = dot(arrived_ref[pl.ds(0, peers, stride=2), :].astype(BF16), place, (0, 0))
    keep = (iota(spread.shape, 1) & 3) == (iota(spread.shape, 0) >> 5)
    spread = jnp.where(keep, spread, 0.0)
    parents = spread[:32] + spread[32:64] + spread[64:96] + spread[96:]
    parents_ref[...] = parents.astype(BF16)


def parents_of(arrived, slots):
    return pl.pallas_call(
        parents_kernel,
        name="parents",
        out_shape=jax.ShapeDtypeStruct((32, slots), BF16),
        compiler_params=pltpu.CompilerParams(vmem_limit_bytes=SMALL_BYTES),
    )(arrived)


def finish_kernel(total_ref, out_ref):
    kids, outs, width = out_ref.shape
    for kid in range(kids):
        rows = slice(kid // 2 * outs, (kid // 2 + 1) * outs)
        out_ref[kid] = total_ref[rows, kid % 2 * width : (kid % 2 + 1) * width]


def finish(total, width):
    return pl.pallas_call(
        finish_kernel,
        name="finish",
        out_shape=jax.ShapeDtypeStruct((KIDS, 32, width), F32),
        compiler_params=pltpu.CompilerParams(vmem_limit_bytes=SMALL_BYTES),
    )(total)


def first_of(peers):
    return peers * 9 // 16


def exchange(array, axis):
    peers = lax.axis_size(axis)
    order = [(i + first_of(peers)) % peers for i in range(peers)]
    return lax.all_to_all(array, axis, 0, 0, axis_index_groups=[order], tiled=True)


def per_device(features, neighbours, child_count, dest, conv_weight, merge_weight, parent_grad):
    chans, peers = lax.axis_size("chan"), lax.axis_size("leaf")
    width, rows = features.shape
    slots = parent_grad.shape[1]
    weights = exchange(pack(jnp.swapaxes(conv_weight, 1, 2), chans), "chan")
    edge, grad_out = cut(features, parent_grad, peers)
    pairs = [(p * chans, (p + 1) * chans) for p in range(peers - 1)]
    pairs += [((p + 1) * chans + chans - 1, p * chans + chans - 1) for p in range(peers - 1)]
    halo = lax.ppermute(edge, ("leaf", "chan"), pairs)
    weights, grad_out = lax.optimization_barrier((weights, grad_out))
    returned = exchange(grad_out, "leaf")

    owner = (dest // slots + peers - first_of(peers)) % peers
    owner = jnp.where(dest >= 0, owner, -1)
    owner = owner.reshape(slots // 32, 8, 4).transpose(0, 2, 1).reshape(1, slots)
    merge_all = jnp.tile(merge_weight.reshape(KIDS * width, 32), (1, 4))

    hidden = exchange(conv(child_count, features, halo, neighbours, weights), "chan")
    outbox = merge(*fetch(owner, returned), hidden, merge_all).reshape(peers, 2, 128)
    arrived = exchange(outbox, "leaf").reshape(2 * peers, 128)
    total = total_of(arrived, 1.0 / math.sqrt(rows))
    parents = parents_of(arrived, slots)
    grad = finish(exchange(total, "leaf"), width)
    return parents, grad.swapaxes(1, 2)


def solution(mesh):
    in_specs = (
        P(None, "leaf"),
        P(None, "leaf"),
        P("leaf"),
        P("leaf"),
        P(None, None, "chan"),
        P(None, None, "chan"),
        P("chan", "leaf"),
    )
    out_specs = (P("chan", "leaf"), P(None, None, "chan"))
    return jax.shard_map(
        per_device, mesh=mesh, in_specs=in_specs, out_specs=out_specs, check_vma=False
    )
```

```python
import functools
import math

import jax
import jax.numpy as jnp
from jax import lax
from jax.experimental import pallas as pl
from jax.experimental.pallas import tpu as pltpu
from jax.sharding import PartitionSpec as P

KIDS = 8
HALO = 1024
BLOCK = 256
VMEM_BYTES = 24 << 20
SMALL_BYTES = 8 << 20
LARGE_BYTES = 56 << 20

BF16 = jnp.bfloat16
F32 = jnp.float32


def dot(a, b, contract):
    return lax.dot_general(a, b, ((contract[:1], contract[1:]), ((), ())), preferred_element_type=F32)


def iota(shape, dim):
    return lax.broadcasted_iota(jnp.int32, shape, dim)


def one_hot(hit):
    return jnp.where(hit, 1.0, 0.0).astype(BF16)


def conv_kernel(
    count_ref,
    features_ref,
    halo_ref,
    offsets_ref,
    weights_ref,
    out_ref,
    window,
    weight,
    gathered,
    swap,
):
    channel, valid_rows = lax.axis_index("chan"), count_ref[0]
    width = features_ref.shape[0]
    taps = offsets_ref.shape[0]
    chans = features_ref.shape[1] // HALO
    halo_pieces = HALO // BLOCK
    pieces = window.shape[0] // width
    reach = (2 * HALO) // BLOCK + 1

    for i in range(pieces):
        at = channel * halo_pieces + i - halo_pieces
        last = features_ref.shape[1] // BLOCK - 1
        inside = jnp.clip(at, 0, last) * BLOCK
        own = features_ref[:, pl.ds(pl.multiple_of(inside, BLOCK), BLOCK)]
        other = halo_ref[:, (i % halo_pieces) * BLOCK : (i % halo_pieces + 1) * BLOCK]
        outside = (at < 0) | (at > last)
        window[i * width : (i + 1) * width, :] = jnp.where(outside, other, own)
    half, part = (taps + 1) // 2, width // chans
    for source in range(chans):
        for tap in range(taps):
            rows = slice(tap % half * part, (tap % half + 1) * part)
            value = weights_ref[(source - first_of(chans)) % chans, rows, tap // half * width : (tap // half + 1) * width]
            weight[source * part : (source + 1) * part, tap * width : (tap + 1) * width] = value
    row, lane = iota((BLOCK, BLOCK), 0), iota((BLOCK, BLOCK), 1)
    kid, slot, group = row & 7, (row >> 3) & 3, row >> 5
    swap[...] = one_hot(lane == kid * 32 + slot * 8 + group)

    middle = taps // 2
    counted = lax.broadcasted_iota(jnp.int16, (BLOCK, BLOCK), 0)
    one, zero = jnp.ones((BLOCK, BLOCK), BF16), jnp.zeros((BLOCK, BLOCK), BF16)
    steps = HALO // BLOCK

    def gather(step, tap, low, high):
        slot, rows = step % 2, slice(tap * width, (tap + 1) * width)
        if tap == middle:
            centre = (step + halo_pieces) * width
            gathered[slot, rows, :] = window[centre : centre + width, :]
            return
        hit = jnp.where(counted == low[tap : tap + 1, :].astype(jnp.int16), one, zero)
        found = dot(window[step * width : (step + reach) * width, :], hit, (1, 0))
        block = high[tap : tap + 1, :]
        total = found[:width]
        for k in range(1, reach):
            total = jnp.where(block == k, found[k * width : (k + 1) * width], total)
        gathered[slot, rows, :] = total.astype(BF16)

    def activate(step):
        pre_act = dot(weight[...], gathered[step % 2], (1, 0))
        row = channel * HALO + step * BLOCK + iota((1, BLOCK), 1)
        return jnp.where(row < valid_rows, jnp.maximum(pre_act, 0.0), 0.0).astype(BF16)

    hidden = []
    for step in range(steps):
        start = pl.multiple_of(channel * HALO + step * BLOCK, BLOCK)
        offsets = offsets_ref[:, pl.ds(start, BLOCK)]
        at = offsets + iota(offsets.shape, 1)
        low = jnp.where(offsets >= 0, at & (BLOCK - 1), -1)
        high = at >> 8
        for tap in range(taps):
            gather(step, tap, low, high)
            if step > 0 and tap == 2:
                hidden.append(activate(step - 1))
    hidden.append(activate(steps - 1))
    spread = dot(jnp.concatenate(hidden, axis=0), swap[...], (1, 0))
    group = iota((width, 128), 1) >> 5
    for kid in range(KIDS):
        total = None
        for step in range(steps):
            half = spread[step * width : (step + 1) * width, kid // 4 * 128 : (kid // 4 + 1) * 128]
            shift = (32 * step + 128 - 32 * (kid % 4)) % 128
            moved = pltpu.roll(half, shift, axis=1) if shift else half
            total = moved if total is None else jnp.where(group == step, moved, total)
        rows = slice(kid * width, (kid + 1) * width)
        for peer in range(out_ref.shape[0]):
            out_ref[peer, rows, :] = total.astype(BF16)


def conv(count, features, halo, offsets, weights):
    width = features.shape[0]
    taps = offsets.shape[0]
    vmem = pl.BlockSpec(memory_space=pltpu.VMEM)
    return pl.pallas_call(
        conv_kernel,
        name="conv",
        out_shape=jax.ShapeDtypeStruct((weights.shape[0], KIDS * width, HALO // KIDS), BF16),
        in_specs=[
            pl.BlockSpec(memory_space=pltpu.SMEM),
            vmem,
            vmem,
            vmem,
            vmem,
        ],
        out_specs=vmem,
        scratch_shapes=[
            pltpu.VMEM((3 * HALO // BLOCK * width, BLOCK), BF16),
            pltpu.VMEM((width, taps * width), BF16),
            pltpu.VMEM((2, taps * width, BLOCK), BF16),
            pltpu.VMEM((BLOCK, BLOCK), BF16),
        ],
        compiler_params=pltpu.CompilerParams(vmem_limit_bytes=VMEM_BYTES),
        cost_estimate=pl.CostEstimate(flops=8_000_000_000, bytes_accessed=2_000_000, transcendentals=0),
    )(count, features, halo, offsets, weights)


def pack_kernel(weight_ref, out_ref):
    taps, part, width = weight_ref.shape
    half = (taps + 1) // 2
    out_ref[0, (half - 1) * part :, width:] = jnp.zeros((part, width), BF16)
    for tap in range(taps):
        rows = slice(tap % half * part, (tap % half + 1) * part)
        out_ref[0, rows, tap // half * width : (tap // half + 1) * width] = weight_ref[tap]
    packed = out_ref[0]
    for peer in range(1, out_ref.shape[0]):
        out_ref[peer] = packed


def pack(weight, chans):
    taps, part, width = weight.shape
    return pl.pallas_call(
        pack_kernel,
        name="pack",
        out_shape=jax.ShapeDtypeStruct((chans, (taps + 1) // 2 * part, 2 * width), BF16),
        in_specs=[pl.BlockSpec(memory_space=pltpu.VMEM)],
        out_specs=pl.BlockSpec(memory_space=pltpu.VMEM),
        compiler_params=pltpu.CompilerParams(vmem_limit_bytes=SMALL_BYTES),
    )(weight)


def cut_kernel(features_hbm, grad_hbm, edge_ref, cut_ref, grad_ref, edge_arrival, grad_arrival):
    peers, slots = cut_ref.shape[0], grad_ref.shape[1]
    last = features_hbm.shape[1] - HALO
    start = pl.multiple_of(jnp.where(lax.axis_index("chan") == 0, last, 0), HALO)
    edge_copy = pltpu.make_async_copy(features_hbm.at[:, pl.ds(start, HALO)], edge_ref, edge_arrival)
    grad_copy = pltpu.make_async_copy(grad_hbm, grad_ref, grad_arrival)
    edge_copy.start()
    grad_copy.start()
    peer = lax.rem(iota((peers, slots), 0) + cut_first_of(peers), peers)
    where = one_hot((iota((peers, slots), 1) >> 2) == peer)
    grad_copy.wait()
    grad = jnp.concatenate([grad_ref[...]] * 4, axis=0).astype(F32)
    keep = (iota(grad.shape, 1) & 3) == (iota(grad.shape, 0) >> 5)
    grad = jnp.where(keep, grad, 0.0).astype(BF16)
    cut_ref[...] = dot(where, grad, (1, 1))
    edge_copy.wait()


def cut(features, parent_grad, peers):
    hbm = pl.BlockSpec(memory_space=pl.ANY)
    return pl.pallas_call(
        cut_kernel,
        name="cut",
        out_shape=(
            jax.ShapeDtypeStruct((features.shape[0], HALO), BF16),
            jax.ShapeDtypeStruct((peers, 128), F32),
        ),
        in_specs=[hbm, hbm],
        scratch_shapes=[
            pltpu.VMEM(parent_grad.shape, BF16),
            pltpu.SemaphoreType.DMA,
            pltpu.SemaphoreType.DMA,
        ],
        compiler_params=pltpu.CompilerParams(vmem_limit_bytes=LARGE_BYTES),
    )(features, parent_grad)


def fetch_kernel(owner_ref, returned_ref, place_ref, fetched_ref):
    place = one_hot(iota(place_ref.shape, 0) == owner_ref[...])
    place_ref[...] = place
    peers = returned_ref.shape[0]
    turn = (first_of(peers) - cut_first_of(peers)) % peers
    returned = jnp.concatenate([returned_ref[turn:], returned_ref[:turn]], axis=0)
    fetched = dot(place, returned.astype(BF16), (0, 0))
    own = ((iota(fetched.shape, 0) >> 3) & 3) == (iota(fetched.shape, 1) >> 5)
    fetched = jnp.where(own, fetched, 0.0)
    fetched = fetched + pltpu.roll(fetched, 64, axis=1)
    fetched = fetched + pltpu.roll(fetched, 32, axis=1)
    fetched_ref[...] = fetched.astype(BF16)


def fetch(owner, returned):
    peers, slots = returned.shape[0], owner.shape[1]
    return pl.pallas_call(
        fetch_kernel,
        name="fetch",
        out_shape=(
            jax.ShapeDtypeStruct((peers, slots), BF16),
            jax.ShapeDtypeStruct((slots, 128), BF16),
        ),
        compiler_params=pltpu.CompilerParams(vmem_limit_bytes=SMALL_BYTES),
    )(owner, returned)


def merge_kernel(place_ref, fetched_ref, hidden_ref, weight_ref, out_ref):
    peers, slots = place_ref.shape
    count, depth = hidden_ref.shape[:2]
    share = slots // count
    own = ((iota((share, 128), 0) >> 3) & 3) == (iota((share, 128), 1) >> 5)
    outbox = jnp.zeros((peers, 128), F32)
    grad = jnp.zeros((128, depth), F32)
    for piece in range(count):
        hidden = hidden_ref[piece]
        quarter = (piece + first_of(count)) % count
        rows = slice(quarter * share, (quarter + 1) * share)
        merged = dot(hidden, weight_ref[...], (0, 0))
        merged = jnp.where(own, merged, 0.0).astype(BF16)
        outbox = outbox + dot(place_ref[:, rows], merged, (1, 0))
        grad = grad + dot(fetched_ref[rows, :], hidden, (0, 1))
    out_ref[pl.ds(0, peers, stride=2), :] = outbox
    for k in range(depth // 128):
        out_ref[pl.ds(64 * k + 1, 32, stride=2), :] = grad[:32, k * 128 : (k + 1) * 128]


def merge(place, fetched, hidden, weight):
    return pl.pallas_call(
        merge_kernel,
        name="merge",
        out_shape=jax.ShapeDtypeStruct((2 * place.shape[0], 128), F32),
        compiler_params=pltpu.CompilerParams(vmem_limit_bytes=SMALL_BYTES),
    )(place, fetched, hidden, weight)


def total_kernel(scale, arrived_ref, total_ref):
    peers = total_ref.shape[0]
    total = jnp.sum(arrived_ref[pl.ds(1, peers, stride=2), :], axis=0, keepdims=True) * scale
    total_ref[...] = jnp.broadcast_to(total, total_ref.shape)


def total_of(arrived, scale):
    return pl.pallas_call(
        functools.partial(total_kernel, scale),
        name="total",
        out_shape=jax.ShapeDtypeStruct((arrived.shape[0] // 2, 128), F32),
        compiler_params=pltpu.CompilerParams(vmem_limit_bytes=SMALL_BYTES),
    )(arrived)


def parents_kernel(arrived_ref, parents_ref):
    peers, slots = arrived_ref.shape[0] // 2, parents_ref.shape[1]
    peer = lax.rem(iota((peers, slots), 0) + first_of(peers), peers)
    place = one_hot((iota((peers, slots), 1) >> 2) == peer)
    spread = dot(arrived_ref[pl.ds(0, peers, stride=2), :].astype(BF16), place, (0, 0))
    keep = (iota(spread.shape, 1) & 3) == (iota(spread.shape, 0) >> 5)
    spread = jnp.where(keep, spread, 0.0)
    parents = spread[:32] + spread[32:64] + spread[64:96] + spread[96:]
    parents_ref[...] = parents.astype(BF16)


def parents_of(arrived, slots):
    return pl.pallas_call(
        parents_kernel,
        name="parents",
        out_shape=jax.ShapeDtypeStruct((32, slots), BF16),
        compiler_params=pltpu.CompilerParams(vmem_limit_bytes=SMALL_BYTES),
    )(arrived)


def finish_kernel(total_ref, out_ref):
    kids, outs, width = out_ref.shape
    for kid in range(kids):
        rows = slice(kid // 2 * outs, (kid // 2 + 1) * outs)
        out_ref[kid] = total_ref[rows, kid % 2 * width : (kid % 2 + 1) * width]


def finish(total, width):
    return pl.pallas_call(
        finish_kernel,
        name="finish",
        out_shape=jax.ShapeDtypeStruct((KIDS, 32, width), F32),
        compiler_params=pltpu.CompilerParams(vmem_limit_bytes=SMALL_BYTES),
    )(total)


def first_of(peers):
    return peers * 9 // 16


def cut_first_of(peers):
    return peers * 13 // 16


def exchange(array, axis, first=None):
    peers = lax.axis_size(axis)
    first = first_of(peers) if first is None else first
    order = [(i + first) % peers for i in range(peers)]
    return lax.all_to_all(array, axis, 0, 0, axis_index_groups=[order], tiled=True)


def per_device(features, neighbours, child_count, dest, conv_weight, merge_weight, parent_grad):
    chans, peers = lax.axis_size("chan"), lax.axis_size("leaf")
    width, rows = features.shape
    slots = parent_grad.shape[1]
    weights = exchange(pack(jnp.swapaxes(conv_weight, 1, 2), chans), "chan")
    edge, grad_out = cut(features, parent_grad, peers)
    pairs = [(p * chans, (p + 1) * chans) for p in range(peers - 1)]
    pairs += [((p + 1) * chans + chans - 1, p * chans + chans - 1) for p in range(peers - 1)]
    halo = lax.ppermute(edge, ("leaf", "chan"), pairs)
    weights, grad_out = lax.optimization_barrier((weights, grad_out))
    returned = exchange(grad_out, "leaf", cut_first_of(peers))

    owner = (dest // slots + peers - first_of(peers)) % peers
    owner = jnp.where(dest >= 0, owner, -1)
    owner = owner.reshape(slots // 32, 8, 4).transpose(0, 2, 1).reshape(1, slots)
    merge_all = jnp.tile(merge_weight.reshape(KIDS * width, 32), (1, 4))

    hidden = exchange(conv(child_count, features, halo, neighbours, weights), "chan")
    outbox = merge(*fetch(owner, returned), hidden, merge_all).reshape(peers, 2, 128)
    arrived = exchange(outbox, "leaf").reshape(2 * peers, 128)
    total = total_of(arrived, 1.0 / math.sqrt(rows))
    parents = parents_of(arrived, slots)
    grad = finish(exchange(total, "leaf"), width)
    return parents, grad.swapaxes(1, 2)


def solution(mesh):
    in_specs = (
        P(None, "leaf"),
        P(None, "leaf"),
        P("leaf"),
        P("leaf"),
        P(None, None, "chan"),
        P(None, None, "chan"),
        P("chan", "leaf"),
    )
    out_specs = (P("chan", "leaf"), P(None, None, "chan"))
    return jax.shard_map(
        per_device, mesh=mesh, in_specs=in_specs, out_specs=out_specs, check_vma=False
    )
```

```python
import functools
import math

import jax
import jax.numpy as jnp
from jax import lax
from jax.experimental import pallas as pl
from jax.experimental.pallas import tpu as pltpu
from jax.sharding import PartitionSpec as P

KIDS = 8
HALO = 1024
BLOCK = 256
VMEM_BYTES = 24 << 20
SMALL_BYTES = 8 << 20
LARGE_BYTES = 56 << 20

BF16 = jnp.bfloat16
F32 = jnp.float32


def dot(a, b, contract):
    return lax.dot_general(a, b, ((contract[:1], contract[1:]), ((), ())), preferred_element_type=F32)


def iota(shape, dim):
    return lax.broadcasted_iota(jnp.int32, shape, dim)


def one_hot(hit):
    return jnp.where(hit, 1.0, 0.0).astype(BF16)


def conv_kernel(
    count_ref,
    features_ref,
    halo_ref,
    offsets_ref,
    weights_ref,
    out_ref,
    window,
    weight,
    gathered,
    swap,
):
    channel, valid_rows = lax.axis_index("chan"), count_ref[0]
    width = features_ref.shape[0]
    taps = offsets_ref.shape[0]
    chans = features_ref.shape[1] // HALO
    halo_pieces = HALO // BLOCK
    pieces = window.shape[0] // width
    reach = (2 * HALO) // BLOCK + 1

    for i in range(pieces):
        at = channel * halo_pieces + i - halo_pieces
        last = features_ref.shape[1] // BLOCK - 1
        inside = jnp.clip(at, 0, last) * BLOCK
        own = features_ref[:, pl.ds(pl.multiple_of(inside, BLOCK), BLOCK)]
        other = halo_ref[:, (i % halo_pieces) * BLOCK : (i % halo_pieces + 1) * BLOCK]
        outside = (at < 0) | (at > last)
        window[i * width : (i + 1) * width, :] = jnp.where(outside, other, own)
    half, part = (taps + 1) // 2, width // chans
    for source in range(chans):
        for tap in range(taps):
            rows = slice(tap % half * part, (tap % half + 1) * part)
            value = weights_ref[(source - first_of(chans)) % chans, rows, tap // half * width : (tap // half + 1) * width]
            weight[source * part : (source + 1) * part, tap * width : (tap + 1) * width] = value
    row, lane = iota((BLOCK, BLOCK), 0), iota((BLOCK, BLOCK), 1)
    kid, slot, group = row & 7, (row >> 3) & 3, row >> 5
    swap[...] = one_hot(lane == kid * 32 + slot * 8 + group)

    middle = taps // 2
    counted = lax.broadcasted_iota(jnp.int16, (BLOCK, BLOCK), 0)
    one, zero = jnp.ones((BLOCK, BLOCK), BF16), jnp.zeros((BLOCK, BLOCK), BF16)
    steps = HALO // BLOCK

    def gather(step, tap, low, high):
        slot, rows = step % 2, slice(tap * width, (tap + 1) * width)
        if tap == middle:
            centre = (step + halo_pieces) * width
            gathered[slot, rows, :] = window[centre : centre + width, :]
            return
        hit = jnp.where(counted == low[tap : tap + 1, :].astype(jnp.int16), one, zero)
        found = dot(window[step * width : (step + reach) * width, :], hit, (1, 0))
        block = high[tap : tap + 1, :]
        total = found[:width]
        for k in range(1, reach):
            total = jnp.where(block == k, found[k * width : (k + 1) * width], total)
        gathered[slot, rows, :] = total.astype(BF16)

    def activate(step):
        pre_act = dot(weight[...], gathered[step % 2], (1, 0))
        row = channel * HALO + step * BLOCK + iota((1, BLOCK), 1)
        return jnp.where(row < valid_rows, jnp.maximum(pre_act, 0.0), 0.0).astype(BF16)

    hidden = []
    for step in range(steps):
        start = pl.multiple_of(channel * HALO + step * BLOCK, BLOCK)
        offsets = offsets_ref[:, pl.ds(start, BLOCK)]
        at = offsets + iota(offsets.shape, 1)
        low = jnp.where(offsets >= 0, at & (BLOCK - 1), -1)
        high = at >> 8
        for tap in range(taps):
            gather(step, tap, low, high)
            if step > 0 and tap == 2:
                hidden.append(activate(step - 1))
    hidden.append(activate(steps - 1))
    spread = dot(jnp.concatenate(hidden, axis=0), swap[...], (1, 0))
    group = iota((width, 128), 1) >> 5
    for kid in range(KIDS):
        total = None
        for step in range(steps):
            half = spread[step * width : (step + 1) * width, kid // 4 * 128 : (kid // 4 + 1) * 128]
            shift = (32 * step + 128 - 32 * (kid % 4)) % 128
            moved = pltpu.roll(half, shift, axis=1) if shift else half
            total = moved if total is None else jnp.where(group == step, moved, total)
        rows = slice(kid * width, (kid + 1) * width)
        for peer in range(out_ref.shape[0]):
            out_ref[peer, rows, :] = total.astype(BF16)


def conv(count, features, halo, offsets, weights):
    width = features.shape[0]
    taps = offsets.shape[0]
    vmem = pl.BlockSpec(memory_space=pltpu.VMEM)
    return pl.pallas_call(
        conv_kernel,
        name="conv",
        out_shape=jax.ShapeDtypeStruct((weights.shape[0], KIDS * width, HALO // KIDS), BF16),
        in_specs=[
            pl.BlockSpec(memory_space=pltpu.SMEM),
            vmem,
            vmem,
            vmem,
            vmem,
        ],
        out_specs=vmem,
        scratch_shapes=[
            pltpu.VMEM((3 * HALO // BLOCK * width, BLOCK), BF16),
            pltpu.VMEM((width, taps * width), BF16),
            pltpu.VMEM((2, taps * width, BLOCK), BF16),
            pltpu.VMEM((BLOCK, BLOCK), BF16),
        ],
        compiler_params=pltpu.CompilerParams(vmem_limit_bytes=VMEM_BYTES),
        cost_estimate=pl.CostEstimate(flops=8_000_000_000, bytes_accessed=2_000_000, transcendentals=0),
    )(count, features, halo, offsets, weights)


def pack_kernel(weight_ref, out_ref):
    taps, part, width = weight_ref.shape
    half = (taps + 1) // 2
    out_ref[0, (half - 1) * part :, width:] = jnp.zeros((part, width), BF16)
    for tap in range(taps):
        rows = slice(tap % half * part, (tap % half + 1) * part)
        out_ref[0, rows, tap // half * width : (tap // half + 1) * width] = weight_ref[tap]
    packed = out_ref[0]
    for peer in range(1, out_ref.shape[0]):
        out_ref[peer] = packed


def pack(weight, chans):
    taps, part, width = weight.shape
    return pl.pallas_call(
        pack_kernel,
        name="pack",
        out_shape=jax.ShapeDtypeStruct((chans, (taps + 1) // 2 * part, 2 * width), BF16),
        in_specs=[pl.BlockSpec(memory_space=pltpu.VMEM)],
        out_specs=pl.BlockSpec(memory_space=pltpu.VMEM),
        compiler_params=pltpu.CompilerParams(vmem_limit_bytes=SMALL_BYTES),
    )(weight)


def cut_kernel(features_hbm, grad_hbm, edge_ref, cut_ref, grad_ref, edge_arrival, grad_arrival):
    peers, slots = cut_ref.shape[0], grad_ref.shape[1]
    last = features_hbm.shape[1] - HALO
    start = pl.multiple_of(jnp.where(lax.axis_index("chan") == 0, last, 0), HALO)
    edge_copy = pltpu.make_async_copy(features_hbm.at[:, pl.ds(start, HALO)], edge_ref, edge_arrival)
    grad_copy = pltpu.make_async_copy(grad_hbm, grad_ref, grad_arrival)
    edge_copy.start()
    grad_copy.start()
    peer = lax.rem(iota((peers, slots), 0) + cut_first_of(peers), peers)
    where = one_hot((iota((peers, slots), 1) >> 2) == peer)
    grad_copy.wait()
    grad = jnp.concatenate([grad_ref[...]] * 4, axis=0).astype(F32)
    keep = (iota(grad.shape, 1) & 3) == (iota(grad.shape, 0) >> 5)
    grad = jnp.where(keep, grad, 0.0).astype(BF16)
    cut_ref[...] = dot(where, grad, (1, 1))
    edge_copy.wait()


def cut(features, parent_grad, peers):
    hbm = pl.BlockSpec(memory_space=pl.ANY)
    return pl.pallas_call(
        cut_kernel,
        name="cut",
        out_shape=(
            jax.ShapeDtypeStruct((features.shape[0], HALO), BF16),
            jax.ShapeDtypeStruct((peers, 128), F32),
        ),
        in_specs=[hbm, hbm],
        scratch_shapes=[
            pltpu.VMEM(parent_grad.shape, BF16),
            pltpu.SemaphoreType.DMA,
            pltpu.SemaphoreType.DMA,
        ],
        compiler_params=pltpu.CompilerParams(vmem_limit_bytes=LARGE_BYTES),
    )(features, parent_grad)


def fetch_kernel(owner_ref, returned_ref, place_ref, fetched_ref):
    place = one_hot(iota(place_ref.shape, 0) == owner_ref[...])
    place_ref[...] = place
    peers = returned_ref.shape[0]
    turn = (first_of(peers) - cut_first_of(peers)) % peers
    returned = jnp.concatenate([returned_ref[turn:], returned_ref[:turn]], axis=0)
    fetched = dot(place, returned.astype(BF16), (0, 0))
    own = ((iota(fetched.shape, 0) >> 3) & 3) == (iota(fetched.shape, 1) >> 5)
    fetched = jnp.where(own, fetched, 0.0)
    fetched = fetched + pltpu.roll(fetched, 64, axis=1)
    fetched = fetched + pltpu.roll(fetched, 32, axis=1)
    fetched_ref[...] = fetched.astype(BF16)


def fetch(owner, returned):
    peers, slots = returned.shape[0], owner.shape[1]
    return pl.pallas_call(
        fetch_kernel,
        name="fetch",
        out_shape=(
            jax.ShapeDtypeStruct((peers, slots), BF16),
            jax.ShapeDtypeStruct((slots, 128), BF16),
        ),
        compiler_params=pltpu.CompilerParams(vmem_limit_bytes=SMALL_BYTES),
    )(owner, returned)


def merge_kernel(place_ref, fetched_ref, hidden_ref, weight_ref, out_ref):
    peers, slots = place_ref.shape
    count, depth = hidden_ref.shape[:2]
    share = slots // count
    own = ((iota((share, 128), 0) >> 3) & 3) == (iota((share, 128), 1) >> 5)
    outbox = jnp.zeros((peers, 128), F32)
    grad = jnp.zeros((128, depth), F32)
    for piece in range(count):
        hidden = hidden_ref[piece]
        quarter = (piece + first_of(count)) % count
        rows = slice(quarter * share, (quarter + 1) * share)
        merged = dot(hidden, weight_ref[...], (0, 0))
        merged = jnp.where(own, merged, 0.0).astype(BF16)
        outbox = outbox + dot(place_ref[:, rows], merged, (1, 0))
        grad = grad + dot(fetched_ref[rows, :], hidden, (0, 1))
    out_ref[pl.ds(0, peers, stride=2), :] = outbox
    for k in range(depth // 128):
        out_ref[pl.ds(64 * k + 1, 32, stride=2), :] = grad[:32, k * 128 : (k + 1) * 128]


def merge(place, fetched, hidden, weight):
    return pl.pallas_call(
        merge_kernel,
        name="merge",
        out_shape=jax.ShapeDtypeStruct((2 * place.shape[0], 128), F32),
        compiler_params=pltpu.CompilerParams(vmem_limit_bytes=SMALL_BYTES),
    )(place, fetched, hidden, weight)


def total_kernel(scale, arrived_ref, total_ref):
    peers = total_ref.shape[0]
    total = jnp.sum(arrived_ref[pl.ds(1, peers, stride=2), :], axis=0, keepdims=True) * scale
    total_ref[...] = jnp.broadcast_to(total, total_ref.shape)


def total_of(arrived, scale):
    return pl.pallas_call(
        functools.partial(total_kernel, scale),
        name="total",
        out_shape=jax.ShapeDtypeStruct((arrived.shape[0] // 2, 128), F32),
        compiler_params=pltpu.CompilerParams(vmem_limit_bytes=SMALL_BYTES),
    )(arrived)


def parents_kernel(arrived_ref, parents_ref):
    peers, slots = arrived_ref.shape[0] // 2, parents_ref.shape[1]
    peer = lax.rem(iota((peers, slots), 0) + first_of(peers), peers)
    place = one_hot((iota((peers, slots), 1) >> 2) == peer)
    spread = dot(arrived_ref[pl.ds(0, peers, stride=2), :].astype(BF16), place, (0, 0))
    keep = (iota(spread.shape, 1) & 3) == (iota(spread.shape, 0) >> 5)
    spread = jnp.where(keep, spread, 0.0)
    parents = spread[:32] + spread[32:64] + spread[64:96] + spread[96:]
    parents_ref[...] = parents.astype(BF16)


def parents_of(arrived, slots):
    return pl.pallas_call(
        parents_kernel,
        name="parents",
        out_shape=jax.ShapeDtypeStruct((32, slots), BF16),
        compiler_params=pltpu.CompilerParams(vmem_limit_bytes=SMALL_BYTES),
    )(arrived)


def finish_kernel(total_ref, out_ref):
    kids, outs, width = out_ref.shape
    for kid in range(kids):
        rows = slice(kid // 2 * outs, (kid // 2 + 1) * outs)
        out_ref[kid] = total_ref[rows, kid % 2 * width : (kid % 2 + 1) * width]


def finish(total, width):
    return pl.pallas_call(
        finish_kernel,
        name="finish",
        out_shape=jax.ShapeDtypeStruct((KIDS, 32, width), F32),
        compiler_params=pltpu.CompilerParams(vmem_limit_bytes=SMALL_BYTES),
    )(total)


def first_of(peers):
    return peers * 9 // 16


def cut_first_of(peers):
    return peers * 27 // 32


def exchange(array, axis, first=None):
    peers = lax.axis_size(axis)
    first = first_of(peers) if first is None else first
    order = [(i + first) % peers for i in range(peers)]
    return lax.all_to_all(array, axis, 0, 0, axis_index_groups=[order], tiled=True)


def per_device(features, neighbours, child_count, dest, conv_weight, merge_weight, parent_grad):
    chans, peers = lax.axis_size("chan"), lax.axis_size("leaf")
    width, rows = features.shape
    slots = parent_grad.shape[1]
    weights = exchange(pack(jnp.swapaxes(conv_weight, 1, 2), chans), "chan")
    edge, grad_out = cut(features, parent_grad, peers)
    pairs = [(p * chans, (p + 1) * chans) for p in range(peers - 1)]
    pairs += [((p + 1) * chans + chans - 1, p * chans + chans - 1) for p in range(peers - 1)]
    halo = lax.ppermute(edge, ("leaf", "chan"), pairs)
    weights, grad_out = lax.optimization_barrier((weights, grad_out))
    returned = exchange(grad_out, "leaf", cut_first_of(peers))

    owner = (dest // slots + peers - first_of(peers)) % peers
    owner = jnp.where(dest >= 0, owner, -1)
    owner = owner.reshape(slots // 32, 8, 4).transpose(0, 2, 1).reshape(1, slots)
    merge_all = jnp.tile(merge_weight.reshape(KIDS * width, 32), (1, 4))

    hidden = exchange(conv(child_count, features, halo, neighbours, weights), "chan")
    outbox = merge(*fetch(owner, returned), hidden, merge_all).reshape(peers, 2, 128)
    arrived = exchange(outbox, "leaf").reshape(2 * peers, 128)
    total = total_of(arrived, 1.0 / math.sqrt(rows))
    parents = parents_of(arrived, slots)
    grad = finish(exchange(total, "leaf"), width)
    return parents, grad.swapaxes(1, 2)


def solution(mesh):
    in_specs = (
        P(None, "leaf"),
        P(None, "leaf"),
        P("leaf"),
        P("leaf"),
        P(None, None, "chan"),
        P(None, None, "chan"),
        P("chan", "leaf"),
    )
    out_specs = (P("chan", "leaf"), P(None, None, "chan"))
    return jax.shard_map(
        per_device, mesh=mesh, in_specs=in_specs, out_specs=out_specs, check_vma=False
    )
```

```python
import functools
import math

import jax
import jax.numpy as jnp
from jax import lax
from jax.experimental import pallas as pl
from jax.experimental.pallas import tpu as pltpu
from jax.sharding import PartitionSpec as P

KIDS = 8
HALO = 1024
BLOCK = 256
VMEM_BYTES = 24 << 20
SMALL_BYTES = 8 << 20
LARGE_BYTES = 56 << 20

BF16 = jnp.bfloat16
F32 = jnp.float32


def dot(a, b, contract):
    return lax.dot_general(a, b, ((contract[:1], contract[1:]), ((), ())), preferred_element_type=F32)


def iota(shape, dim):
    return lax.broadcasted_iota(jnp.int32, shape, dim)


def one_hot(hit):
    return jnp.where(hit, 1.0, 0.0).astype(BF16)


def conv_kernel(
    count_ref,
    features_ref,
    halo_ref,
    offsets_ref,
    weights_ref,
    out_ref,
    window,
    weight,
    gathered,
    swap,
):
    channel, valid_rows = lax.axis_index("chan"), count_ref[0]
    width = features_ref.shape[0]
    taps = offsets_ref.shape[0]
    chans = features_ref.shape[1] // HALO
    halo_pieces = HALO // BLOCK
    pieces = window.shape[0] // width
    reach = (2 * HALO) // BLOCK + 1

    for i in range(pieces):
        at = channel * halo_pieces + i - halo_pieces
        last = features_ref.shape[1] // BLOCK - 1
        inside = jnp.clip(at, 0, last) * BLOCK
        own = features_ref[:, pl.ds(pl.multiple_of(inside, BLOCK), BLOCK)]
        other = halo_ref[:, (i % halo_pieces) * BLOCK : (i % halo_pieces + 1) * BLOCK]
        outside = (at < 0) | (at > last)
        window[i * width : (i + 1) * width, :] = jnp.where(outside, other, own)
    half, part = (taps + 1) // 2, width // chans
    for source in range(chans):
        for tap in range(taps):
            rows = slice(tap % half * part, (tap % half + 1) * part)
            value = weights_ref[(source - first_of(chans)) % chans, rows, tap // half * width : (tap // half + 1) * width]
            weight[source * part : (source + 1) * part, tap * width : (tap + 1) * width] = value
    row, lane = iota((BLOCK, BLOCK), 0), iota((BLOCK, BLOCK), 1)
    kid, slot, group = row & 7, (row >> 3) & 3, row >> 5
    swap[...] = one_hot(lane == kid * 32 + slot * 8 + group)

    middle = taps // 2
    counted = lax.broadcasted_iota(jnp.int16, (BLOCK, BLOCK), 0)
    one, zero = jnp.ones((BLOCK, BLOCK), BF16), jnp.zeros((BLOCK, BLOCK), BF16)
    steps = HALO // BLOCK

    def gather(step, tap, low, high):
        slot, rows = step % 2, slice(tap * width, (tap + 1) * width)
        if tap == middle:
            centre = (step + halo_pieces) * width
            gathered[slot, rows, :] = window[centre : centre + width, :]
            return
        hit = jnp.where(counted == low[tap : tap + 1, :].astype(jnp.int16), one, zero)
        found = dot(window[step * width : (step + reach) * width, :], hit, (1, 0))
        block = high[tap : tap + 1, :]
        total = found[:width]
        for k in range(1, reach):
            total = jnp.where(block == k, found[k * width : (k + 1) * width], total)
        gathered[slot, rows, :] = total.astype(BF16)

    def activate(step):
        pre_act = dot(weight[...], gathered[step % 2], (1, 0))
        row = channel * HALO + step * BLOCK + iota((1, BLOCK), 1)
        return jnp.where(row < valid_rows, jnp.maximum(pre_act, 0.0), 0.0).astype(BF16)

    hidden = []
    for step in range(steps):
        start = pl.multiple_of(channel * HALO + step * BLOCK, BLOCK)
        offsets = offsets_ref[:, pl.ds(start, BLOCK)]
        at = offsets + iota(offsets.shape, 1)
        low = jnp.where(offsets >= 0, at & (BLOCK - 1), -1)
        high = at >> 8
        for tap in range(taps):
            gather(step, tap, low, high)
            if step > 0 and tap == 2:
                hidden.append(activate(step - 1))
    hidden.append(activate(steps - 1))
    spread = dot(jnp.concatenate(hidden, axis=0), swap[...], (1, 0))
    group = iota((width, 128), 1) >> 5
    for kid in range(KIDS):
        total = None
        for step in range(steps):
            half = spread[step * width : (step + 1) * width, kid // 4 * 128 : (kid // 4 + 1) * 128]
            shift = (32 * step + 128 - 32 * (kid % 4)) % 128
            moved = pltpu.roll(half, shift, axis=1) if shift else half
            total = moved if total is None else jnp.where(group == step, moved, total)
        rows = slice(kid * width, (kid + 1) * width)
        for peer in range(out_ref.shape[0]):
            out_ref[peer, rows, :] = total.astype(BF16)


def conv(count, features, halo, offsets, weights):
    width = features.shape[0]
    taps = offsets.shape[0]
    vmem = pl.BlockSpec(memory_space=pltpu.VMEM)
    return pl.pallas_call(
        conv_kernel,
        name="conv",
        out_shape=jax.ShapeDtypeStruct((weights.shape[0], KIDS * width, HALO // KIDS), BF16),
        in_specs=[
            pl.BlockSpec(memory_space=pltpu.SMEM),
            vmem,
            vmem,
            vmem,
            vmem,
        ],
        out_specs=vmem,
        scratch_shapes=[
            pltpu.VMEM((3 * HALO // BLOCK * width, BLOCK), BF16),
            pltpu.VMEM((width, taps * width), BF16),
            pltpu.VMEM((2, taps * width, BLOCK), BF16),
            pltpu.VMEM((BLOCK, BLOCK), BF16),
        ],
        compiler_params=pltpu.CompilerParams(vmem_limit_bytes=VMEM_BYTES),
        cost_estimate=pl.CostEstimate(flops=8_000_000_000, bytes_accessed=2_000_000, transcendentals=0),
    )(count, features, halo, offsets, weights)


def pack_kernel(weight_ref, out_ref):
    taps, part, width = weight_ref.shape
    half = (taps + 1) // 2
    out_ref[0, (half - 1) * part :, width:] = jnp.zeros((part, width), BF16)
    for tap in range(taps):
        rows = slice(tap % half * part, (tap % half + 1) * part)
        out_ref[0, rows, tap // half * width : (tap // half + 1) * width] = weight_ref[tap]
    packed = out_ref[0]
    for peer in range(1, out_ref.shape[0]):
        out_ref[peer] = packed


def pack(weight, chans):
    taps, part, width = weight.shape
    return pl.pallas_call(
        pack_kernel,
        name="pack",
        out_shape=jax.ShapeDtypeStruct((chans, (taps + 1) // 2 * part, 2 * width), BF16),
        in_specs=[pl.BlockSpec(memory_space=pltpu.VMEM)],
        out_specs=pl.BlockSpec(memory_space=pltpu.VMEM),
        compiler_params=pltpu.CompilerParams(vmem_limit_bytes=SMALL_BYTES),
    )(weight)


def cut_kernel(features_hbm, grad_hbm, edge_ref, cut_ref, grad_ref, edge_arrival, grad_arrival):
    peers, slots = cut_ref.shape[0], grad_ref.shape[1]
    last = features_hbm.shape[1] - HALO
    start = pl.multiple_of(jnp.where(lax.axis_index("chan") == 0, last, 0), HALO)
    edge_copy = pltpu.make_async_copy(features_hbm.at[:, pl.ds(start, HALO)], edge_ref, edge_arrival)
    grad_copy = pltpu.make_async_copy(grad_hbm, grad_ref, grad_arrival)
    edge_copy.start()
    grad_copy.start()
    peer = lax.rem(iota((peers, slots), 0) + cut_first_of(peers), peers)
    where = one_hot((iota((peers, slots), 1) >> 2) == peer)
    grad_copy.wait()
    grad = jnp.concatenate([grad_ref[...]] * 4, axis=0).astype(F32)
    keep = (iota(grad.shape, 1) & 3) == (iota(grad.shape, 0) >> 5)
    grad = jnp.where(keep, grad, 0.0).astype(BF16)
    cut_ref[...] = dot(where, grad, (1, 1))
    edge_copy.wait()


def cut(features, parent_grad, peers):
    hbm = pl.BlockSpec(memory_space=pl.ANY)
    return pl.pallas_call(
        cut_kernel,
        name="cut",
        out_shape=(
            jax.ShapeDtypeStruct((features.shape[0], HALO), BF16),
            jax.ShapeDtypeStruct((peers, 128), F32),
        ),
        in_specs=[hbm, hbm],
        scratch_shapes=[
            pltpu.VMEM(parent_grad.shape, BF16),
            pltpu.SemaphoreType.DMA,
            pltpu.SemaphoreType.DMA,
        ],
        compiler_params=pltpu.CompilerParams(vmem_limit_bytes=LARGE_BYTES),
    )(features, parent_grad)


def fetch_kernel(owner_ref, returned_ref, place_ref, fetched_ref):
    place = one_hot(iota(place_ref.shape, 0) == owner_ref[...])
    place_ref[...] = place
    peers = returned_ref.shape[0]
    turn = (first_of(peers) - cut_first_of(peers)) % peers
    returned = jnp.concatenate([returned_ref[turn:], returned_ref[:turn]], axis=0)
    fetched = dot(place, returned.astype(BF16), (0, 0))
    own = ((iota(fetched.shape, 0) >> 3) & 3) == (iota(fetched.shape, 1) >> 5)
    fetched = jnp.where(own, fetched, 0.0)
    fetched = fetched + pltpu.roll(fetched, 64, axis=1)
    fetched = fetched + pltpu.roll(fetched, 32, axis=1)
    fetched_ref[...] = fetched.astype(BF16)


def fetch(owner, returned):
    peers, slots = returned.shape[0], owner.shape[1]
    return pl.pallas_call(
        fetch_kernel,
        name="fetch",
        out_shape=(
            jax.ShapeDtypeStruct((peers, slots), BF16),
            jax.ShapeDtypeStruct((slots, 128), BF16),
        ),
        compiler_params=pltpu.CompilerParams(vmem_limit_bytes=SMALL_BYTES),
    )(owner, returned)


def merge_kernel(place_ref, fetched_ref, hidden_ref, weight_ref, out_ref):
    peers, slots = place_ref.shape
    count, depth = hidden_ref.shape[:2]
    share = slots // count
    own = ((iota((share, 128), 0) >> 3) & 3) == (iota((share, 128), 1) >> 5)
    outbox = jnp.zeros((peers, 128), F32)
    grad = jnp.zeros((128, depth), F32)
    for piece in range(count):
        hidden = hidden_ref[piece]
        rows = slice(piece * share, (piece + 1) * share)
        merged = dot(hidden, weight_ref[...], (0, 0))
        merged = jnp.where(own, merged, 0.0).astype(BF16)
        outbox = outbox + dot(place_ref[:, rows], merged, (1, 0))
        grad = grad + dot(fetched_ref[rows, :], hidden, (0, 1))
    out_ref[pl.ds(0, peers, stride=2), :] = outbox
    for k in range(depth // 128):
        out_ref[pl.ds(64 * k + 1, 32, stride=2), :] = grad[:32, k * 128 : (k + 1) * 128]


def merge(place, fetched, hidden, weight):
    return pl.pallas_call(
        merge_kernel,
        name="merge",
        out_shape=jax.ShapeDtypeStruct((2 * place.shape[0], 128), F32),
        compiler_params=pltpu.CompilerParams(vmem_limit_bytes=SMALL_BYTES),
    )(place, fetched, hidden, weight)


def total_kernel(scale, arrived_ref, total_ref):
    peers = total_ref.shape[0]
    total = jnp.sum(arrived_ref[pl.ds(1, peers, stride=2), :], axis=0, keepdims=True) * scale
    total_ref[...] = jnp.broadcast_to(total, total_ref.shape)


def total_of(arrived, scale):
    return pl.pallas_call(
        functools.partial(total_kernel, scale),
        name="total",
        out_shape=jax.ShapeDtypeStruct((arrived.shape[0] // 2, 128), F32),
        compiler_params=pltpu.CompilerParams(vmem_limit_bytes=SMALL_BYTES),
    )(arrived)


def parents_kernel(arrived_ref, parents_ref):
    peers, slots = arrived_ref.shape[0] // 2, parents_ref.shape[1]
    peer = lax.rem(iota((peers, slots), 0) + first_of(peers), peers)
    place = one_hot((iota((peers, slots), 1) >> 2) == peer)
    spread = dot(arrived_ref[pl.ds(0, peers, stride=2), :].astype(BF16), place, (0, 0))
    keep = (iota(spread.shape, 1) & 3) == (iota(spread.shape, 0) >> 5)
    spread = jnp.where(keep, spread, 0.0)
    parents = spread[:32] + spread[32:64] + spread[64:96] + spread[96:]
    parents_ref[...] = parents.astype(BF16)


def parents_of(arrived, slots):
    return pl.pallas_call(
        parents_kernel,
        name="parents",
        out_shape=jax.ShapeDtypeStruct((32, slots), BF16),
        compiler_params=pltpu.CompilerParams(vmem_limit_bytes=SMALL_BYTES),
    )(arrived)


def finish_kernel(total_ref, out_ref):
    kids, outs, width = out_ref.shape
    for kid in range(kids):
        rows = slice(kid // 2 * outs, (kid // 2 + 1) * outs)
        out_ref[kid] = total_ref[rows, kid % 2 * width : (kid % 2 + 1) * width]


def finish(total, width):
    return pl.pallas_call(
        finish_kernel,
        name="finish",
        out_shape=jax.ShapeDtypeStruct((KIDS, 32, width), F32),
        compiler_params=pltpu.CompilerParams(vmem_limit_bytes=SMALL_BYTES),
    )(total)


def first_of(peers):
    return peers * 9 // 16


def cut_first_of(peers):
    return peers * 27 // 32


def exchange(array, axis, first=None):
    peers = lax.axis_size(axis)
    first = first_of(peers) if first is None else first
    order = [(i + first) % peers for i in range(peers)]
    return lax.all_to_all(array, axis, 0, 0, axis_index_groups=[order], tiled=True)


def per_device(features, neighbours, child_count, dest, conv_weight, merge_weight, parent_grad):
    chans, peers = lax.axis_size("chan"), lax.axis_size("leaf")
    width, rows = features.shape
    slots = parent_grad.shape[1]
    weights = exchange(pack(jnp.swapaxes(conv_weight, 1, 2), chans), "chan")
    edge, grad_out = cut(features, parent_grad, peers)
    pairs = [(p * chans, (p + 1) * chans) for p in range(peers - 1)]
    pairs += [((p + 1) * chans + chans - 1, p * chans + chans - 1) for p in range(peers - 1)]
    halo = lax.ppermute(edge, ("leaf", "chan"), pairs)
    weights, grad_out = lax.optimization_barrier((weights, grad_out))
    returned = exchange(grad_out, "leaf", cut_first_of(peers))

    owner = (dest // slots + peers - first_of(peers)) % peers
    owner = jnp.where(dest >= 0, owner, -1)
    owner = owner.reshape(slots // 32, 8, 4).transpose(0, 2, 1).reshape(1, slots)
    merge_all = jnp.tile(merge_weight.reshape(KIDS * width, 32), (1, 4))

    hidden = exchange(conv(child_count, features, halo, neighbours, weights), "chan", 0)
    outbox = merge(*fetch(owner, returned), hidden, merge_all).reshape(peers, 2, 128)
    arrived = exchange(outbox, "leaf").reshape(2 * peers, 128)
    total = total_of(arrived, 1.0 / math.sqrt(rows))
    parents = parents_of(arrived, slots)
    grad = finish(exchange(total, "leaf"), width)
    return parents, grad.swapaxes(1, 2)


def solution(mesh):
    in_specs = (
        P(None, "leaf"),
        P(None, "leaf"),
        P("leaf"),
        P("leaf"),
        P(None, None, "chan"),
        P(None, None, "chan"),
        P("chan", "leaf"),
    )
    out_specs = (P("chan", "leaf"), P(None, None, "chan"))
    return jax.shard_map(
        per_device, mesh=mesh, in_specs=in_specs, out_specs=out_specs, check_vma=False
    )
```
